256 devices in a mesh: ia: 32 (over z, x_lo, core), ja: 4 (over y), ka: 2 (over x_hi).
Axes of the slice: x: 4 (x_hi: 2, x_lo: 2; x = x_hi * 2 + x_lo), y: 4, z: 8, core: 2. Of those that a mesh axis runs over, the one named last changes fastest.
Arguments:
- tensor: float32 [8192, 8, 8192], P('ja', 'ka', 'ia'), may hold values from -6 to 6
- factor_a: float32 [8192, 128], P('ia'), may hold values from -1 to 1
- factor_c: float32 [8, 128], P('ka'), may hold values from -2 to 2
- gram_c: float32 [128, 128], replicated, may hold values from -12 to 24, as said below
Outputs:
- factor_b: float32 [8192, 128], P('ja')
- factor_c_new: float32 [8, 128], P('ka')
The draws below stay inside these ranges and needn't reach their ends.
Inputs may be any that keep to these rules, and one draw needn't show every extreme that they name: `gram_c`: symmetric positive definite.
All inputs are finite; a program needn't handle non-finite values.
Results may differ from the reference program's by a relative error of at most 0.000071.
Values sent between devices are 32-bit elements; how exact they have to be, the bound alone decides.
No kernel may reach another device: no remote copies, remote signals or barrier semaphores. Data moves between devices by JAX's collectives and lax.ppermute only.
A program may use at most 64 MiB of HBM per device.

```python
import jax
import jax.numpy as jnp
from jax import lax

R = 128
I = 8192
J = 8192
K = 8


def draw_factor_a(key, part):
    first, second, third = jax.random.split(jax.random.fold_in(key, 11), 3)
    noise = jnp.clip(jax.random.normal(first, (I, R), jnp.float32), -4.0, 4.0)
    common = jnp.clip(jax.random.normal(second, (I, 1), jnp.float32), -4.0, 4.0)
    weights = jnp.clip(jax.random.normal(third, (1, R), jnp.float32), -4.0, 4.0)
    return ((noise + 0.7 * common * weights) / jnp.sqrt(jnp.float32(I))).astype(jnp.float32)


def draw_gram_c(key, part):
    first, second = jax.random.split(jax.random.fold_in(key, 23), 2)
    mixing = jnp.clip(jax.random.normal(first, (R, R), jnp.float32), -4.0, 4.0)
    shared = jnp.clip(jax.random.normal(second, (R,), jnp.float32), -3.0, 3.0)
    result = 0.5 * jnp.eye(R, dtype=jnp.float32) + jnp.dot(mixing, mixing.T) / R + 0.3 * jnp.outer(shared, shared)
    return jnp.clip(result, -12.0, 24.0).astype(jnp.float32)


def block_scale(stream_key, extent, pieces, smallest, high):
    def one(axis_at, parts):
        steps = jax.random.uniform(jax.random.fold_in(jax.random.fold_in(stream_key, 6), axis_at), (parts,), jnp.float32, smallest / len(pieces), high / len(pieces))
        return jnp.repeat(jnp.exp(steps), extent[axis_at] // parts).reshape((-1,) + (1,) * (len(extent) - axis_at - 1))

    loudness = one(*pieces[0])
    for cut in pieces[1:]:
        loudness = loudness * one(*cut)
    return loudness


def bell_draw(rng, shape, scale, bound, cuts=(), kind=jnp.bfloat16):
    values = jax.random.normal(rng, shape, jnp.float32) * scale
    if len(cuts) > 0:
        values = block_scale(rng, shape, cuts, -0.22, 0.18) * values
    return jnp.clip(values, min=-bound, max=bound).astype(kind)


def setup_inputs(seed: int = 0) -> dict:
    arg_keys = jax.random.split(jax.random.key(seed), 5)
    tensor = bell_draw(arg_keys[0], (J, K, I), 1.0, 6.0, ((0, 4), (1, 2), (2, 32)), jnp.float32)
    factor_a = draw_factor_a(jax.random.fold_in(arg_keys[4], 71), 0)
    factor_c = bell_draw(arg_keys[2], (K, R), K ** -0.5, 2.0, ((0, 2),), jnp.float32)
    gram_c = draw_gram_c(jax.random.fold_in(arg_keys[4], 71), 0)
    return {"tensor": tensor, "factor_a": factor_a, "factor_c": factor_c, "gram_c": gram_c}


def right_solve(rhs, system):
    lower = jnp.linalg.cholesky(system)
    middle = lax.linalg.triangular_solve(lower, rhs, left_side=False, lower=True, transpose_a=True)
    return lax.linalg.triangular_solve(lower, middle, left_side=False, lower=True, transpose_a=False)

def reference(tensor, factor_a, factor_c, gram_c):
    high = lax.Precision.HIGHEST
    partial_value = jnp.dot(tensor.reshape(J * K, I).astype(jnp.float32), factor_a.astype(jnp.float32), precision=high, preferred_element_type=jnp.float32).reshape(J, K, R)
    gram_a = jnp.dot(factor_a.T.astype(jnp.float32), factor_a.astype(jnp.float32), precision=high, preferred_element_type=jnp.float32)
    mttkrp_b = jnp.sum(partial_value * factor_c[None, :, :], axis=1)
    factor_b = right_solve(mttkrp_b, gram_a * gram_c)
    mttkrp_c = jnp.sum(partial_value * factor_b[:, None, :], axis=0)
    gram_b = jnp.dot(factor_b.T.astype(jnp.float32), factor_b.astype(jnp.float32), precision=high, preferred_element_type=jnp.float32)
    factor_c_new = right_solve(mttkrp_c, gram_a * gram_b)
    return (factor_b, factor_c_new)
```

```python
import jax
import jax.numpy as jnp
from jax import lax
from jax.sharding import Mesh, PartitionSpec as P

HIGH = lax.Precision.HIGHEST
PLANE = ("xl", "xh", "z")


def right_solve(rhs, system):
    lower = jnp.linalg.cholesky(system)
    middle = lax.linalg.triangular_solve(lower, rhs, left_side=False, lower=True, transpose_a=True)
    return lax.linalg.triangular_solve(
        lower, middle, left_side=False, lower=True, transpose_a=False
    )


def swap(x, axis):
    return lax.ppermute(x, axis, [(0, 1), (1, 0)])


def gather(x, axes):
    n = lax.axis_size(axes)
    return lax.all_to_all(jnp.broadcast_to(x[None], (n,) + x.shape), axes, 0, 0)


def body(tensor, factor_a, factor_c, gram_c):
    f32 = jnp.float32
    mode_two, mode_three, mode_one = tensor.shape
    rank = factor_a.shape[1]
    core = lax.axis_index("c")
    plane = lax.axis_size(PLANE)
    pieces = 2 * plane
    rows, extra = mode_two // pieces, rank // pieces

    gram_part = jnp.dot(factor_a.T, factor_a, precision=HIGH, preferred_element_type=f32)
    partial = jnp.dot(
        tensor.reshape(mode_two * mode_three, mode_one),
        factor_a,
        precision=HIGH,
        preferred_element_type=f32,
    ).reshape(mode_two, mode_three, rank)
    part_b = jnp.sum(partial * factor_c[None], axis=1)

    both = jnp.concatenate(
        [
            part_b.reshape(2, plane, rows, rank),
            (0.5 * gram_part).reshape(2, plane, extra, rank),
        ],
        axis=2,
    )
    mine = lax.dynamic_index_in_dim(both, core, 0, keepdims=False)
    other = lax.dynamic_index_in_dim(both, 1 - core, 0, keepdims=False)
    half = mine + swap(other, "c")
    piece = jnp.sum(lax.all_to_all(half, PLANE, 0, 0), axis=0)

    column = gather(piece, "z")
    square = gather(column, ("xl", "xh")).reshape(plane, rows + extra, rank)
    theirs = swap(square, "c")
    first = jnp.where(core == 0, square, theirs)
    second = jnp.where(core == 0, theirs, square)
    whole = jnp.stack([first, second]).reshape(pieces, rows + extra, rank)
    mttkrp_b = whole[:, :rows].reshape(mode_two, rank)
    gram_a = whole[:, rows:].reshape(rank, rank)

    factor_b = right_solve(mttkrp_b, gram_a * gram_c)

    local_c = jnp.sum(partial * factor_b[:, None, :], axis=0)
    local_c = local_c + swap(local_c, "c")
    mttkrp_c = jnp.sum(gather(local_c, ("z", "xl", "y")), axis=0)
    gram_b = jnp.dot(factor_b.T, factor_b, precision=HIGH, preferred_element_type=f32)
    n = lax.axis_size("y")
    away = [lax.ppermute(gram_b, "y", [(i, i ^ k) for i in range(n)]) for k in range(1, n)]
    gram_b = (gram_b + away[0]) + (away[1] + away[2])
    factor_c_new = right_solve(mttkrp_c, gram_a * gram_b)
    return (factor_b, factor_c_new)


def solution(mesh):
    axes = (mesh.shape["ia"] // 4, 2, 2, mesh.shape["ja"], mesh.shape["ka"])
    fine = Mesh(mesh.devices.reshape(axes), ("z", "xl", "c", "y", "xh"))
    split = ("z", "xl", "c")
    placed = (P("y", "xh", split), P(split, None), P("xh", None), P())
    return jax.shard_map(
        body, mesh=fine, in_specs=placed, out_specs=(P("y", None), P("xh", None)), check_vma=False
    )
```

```python
import functools

import jax
import jax.numpy as jnp
from jax import lax
from jax.experimental import pallas as pl
from jax.experimental.pallas import tpu as pltpu
from jax.sharding import Mesh, PartitionSpec as P

HIGH = lax.Precision.HIGHEST
F32 = jnp.float32
PLANE = ("z", "xl", "xh")
VMEM = pl.BlockSpec(memory_space=pltpu.VMEM)


def dot(a, b):
    return jnp.dot(a, b, precision=HIGH, preferred_element_type=F32)


def spd_inverse(a, step):
    n = a.shape[0]
    lane = lax.broadcasted_iota(jnp.int32, (step, n), 1)
    row_of = lax.broadcasted_iota(jnp.int32, (step, n), 0)
    lane_all = lax.broadcasted_iota(jnp.int32, (n, n), 1)
    zero = jnp.zeros((step, n), F32)
    for p in range(0, n, step):
        panel = a[p : p + step]
        columns = [jnp.broadcast_to(panel[:, p + c : p + c + 1], (step, n)) for c in range(step)]
        for c in range(step):
            column = columns[c]
            inverse = 1.0 / jnp.broadcast_to(column[c : c + 1], (step, n))
            pivot = row_of == c

            def eliminate(x):
                row = jnp.broadcast_to(x[c : c + 1], (step, n)) * inverse
                return jnp.where(pivot, row, x - column * row)

            panel = eliminate(jnp.where(lane == p + c, jnp.where(pivot, 1.0, 0.0), panel))
            for q in range(c + 1, step):
                columns[q] = eliminate(columns[q])
        spread = [zero] * (p // step) + [panel] + [zero] * ((n - p) // step - 1)
        rest = jnp.where((lane_all >= p) & (lane_all < p + step), 0.0, a)
        rest = rest - dot(a, jnp.concatenate(spread, axis=0))
        pieces = [rest[:p], panel, rest[p + step :]]
        a = jnp.concatenate([x for x in pieces if x.shape[0]], axis=0)
    return a


def inverse_kernel(first_ref, second_ref, out_ref):
    out_ref[...] = spd_inverse(first_ref[...] * second_ref[...], 16)


def inverse_of_product(first, second):
    return pl.pallas_call(
        inverse_kernel,
        out_shape=jax.ShapeDtypeStruct(first.shape, F32),
        in_specs=[VMEM, VMEM],
        out_specs=VMEM,
        name="inverse_of_product",
    )(first, second)


def swap(x, axis):
    return lax.ppermute(x, axis, [(0, 1), (1, 0)])


def gather(x, axes):
    n = lax.axis_size(axes)
    return lax.all_to_all(jnp.broadcast_to(x[None], (n,) + x.shape), axes, 0, 0)


def body(tensor, factor_a, factor_c, gram_c):
    mode_two, mode_three, mode_one = tensor.shape
    rank = factor_a.shape[1]
    core = lax.axis_index("c")
    plane = lax.axis_size(PLANE)
    pieces = 2 * plane
    rows, extra = mode_two // pieces, rank // pieces

    gram_part = dot(factor_a.T, factor_a)
    partial = dot(tensor.reshape(mode_two * mode_three, mode_one), factor_a)
    partial = partial.reshape(mode_two, mode_three, rank)
    part_b = jnp.sum(partial * factor_c[None], axis=1)

    both = jnp.concatenate(
        [
            part_b.reshape(2, plane, rows, rank),
            (0.5 * gram_part).reshape(2, plane, extra, rank),
        ],
        axis=2,
    )
    mine = lax.dynamic_index_in_dim(both, core, 0, keepdims=False)
    other = lax.dynamic_index_in_dim(both, 1 - core, 0, keepdims=False)
    half = mine + swap(other, "c")
    piece = jnp.sum(lax.all_to_all(half, PLANE, 0, 0), axis=0)

    square = gather(piece, PLANE)
    theirs = swap(square, "c")
    first = jnp.where(core == 0, square, theirs)
    second = jnp.where(core == 0, theirs, square)
    whole = jnp.stack([first, second]).reshape(pieces, rows + extra, rank)
    mttkrp_b = whole[:, :rows].reshape(mode_two, rank)
    gram_a = whole[:, rows:].reshape(rank, rank)

    factor_b = dot(mttkrp_b, inverse_of_product(gram_a, gram_c))

    local_c = jnp.sum(partial * factor_b[:, None, :], axis=0)
    local_c = local_c + swap(local_c, "c")
    mttkrp_c = jnp.sum(gather(local_c, ("z", "xl", "y")), axis=0)
    gram_b = dot(factor_b.T, factor_b)
    n = lax.axis_size("y")
    away = [lax.ppermute(gram_b, "y", [(i, i ^ k) for i in range(n)]) for k in range(1, n)]
    gram_b = (gram_b + away[0]) + (away[1] + away[2])
    factor_c_new = dot(mttkrp_c, inverse_of_product(gram_a, gram_b))
    return (factor_b, factor_c_new)


def solution(mesh):
    axes = (mesh.shape["ia"] // 4, 2, 2, mesh.shape["ja"], mesh.shape["ka"])
    fine = Mesh(mesh.devices.reshape(axes), ("z", "xl", "c", "y", "xh"))
    split = ("z", "xl", "c")
    placed = (P("y", "xh", split), P(split, None), P("xh", None), P())
    return jax.shard_map(
        body, mesh=fine, in_specs=placed, out_specs=(P("y", None), P("xh", None)), check_vma=False
    )
```

```python
import functools

import functools

import jax
import jax.numpy as jnp
from jax import lax
from jax.experimental import pallas as pl
from jax.experimental.pallas import tpu as pltpu
from jax.sharding import Mesh, PartitionSpec as P

HIGH = lax.Precision.HIGHEST
F32 = jnp.float32
BF16 = jnp.bfloat16
PLANE = ("z", "xl", "xh")
VMEM = pl.BlockSpec(memory_space=pltpu.VMEM)


def dot(a, b):
    return jnp.dot(a, b, precision=HIGH, preferred_element_type=F32)


def mxu(a, b):
    return jnp.dot(a, b, preferred_element_type=F32)


def spd_inverse(a, step):
    n = a.shape[0]
    lane = lax.broadcasted_iota(jnp.int32, (step, n), 1)
    row_of = lax.broadcasted_iota(jnp.int32, (step, n), 0)
    lane_all = lax.broadcasted_iota(jnp.int32, (n, n), 1)
    zero = jnp.zeros((step, n), F32)
    for p in range(0, n, step):
        panel = a[p : p + step]
        columns = [jnp.broadcast_to(panel[:, p + c : p + c + 1], (step, n)) for c in range(step)]
        for c in range(step):
            column = columns[c]
            inverse = 1.0 / jnp.broadcast_to(column[c : c + 1], (step, n))
            pivot = row_of == c

            def eliminate(x):
                row = jnp.broadcast_to(x[c : c + 1], (step, n)) * inverse
                return jnp.where(pivot, row, x - column * row)

            panel = eliminate(jnp.where(lane == p + c, jnp.where(pivot, 1.0, 0.0), panel))
            for q in range(c + 1, step):
                columns[q] = eliminate(columns[q])
        spread = [zero] * (p // step) + [panel] + [zero] * ((n - p) // step - 1)
        rest = jnp.where((lane_all >= p) & (lane_all < p + step), 0.0, a)
        rest = rest - dot(a, jnp.concatenate(spread, axis=0))
        pieces = [rest[:p], panel, rest[p + step :]]
        a = jnp.concatenate([x for x in pieces if x.shape[0]], axis=0)
    return a


def inverse_kernel(first_ref, second_ref, out_ref):
    out_ref[...] = spd_inverse(first_ref[...] * second_ref[...], 16)


def inverse_of_product(first, second):
    return pl.pallas_call(
        inverse_kernel,
        out_shape=jax.ShapeDtypeStruct(first.shape, F32),
        in_specs=[VMEM, VMEM],
        out_specs=VMEM,
        name="inverse_of_product",
    )(first, second)


def split3(x):
    high = x.astype(BF16)
    rest = x - high.astype(F32)
    middle = rest.astype(BF16)
    return high, middle, (rest - middle.astype(F32)).astype(BF16)


def contract_kernel(chunk, half_ref, x_hbm, a_ref, c_ref, p_ref, b_ref, x_ref, w_ref, sems):
    count, rows, rank = p_ref.shape
    span = 2 * count
    base = half_ref[0] * (rows * span)
    copies = []
    for n, at in enumerate(range(0, rows, chunk)):
        size = chunk * span
        copy = pltpu.make_async_copy(
            x_hbm.at[pl.ds(base + at * span, size)], x_ref.at[pl.ds(at * span, size)], sems.at[n]
        )
        copy.start()
        copies.append(copy)
    for n, part in enumerate(split3(a_ref[...])):
        w_ref[:, n * rank : (n + 1) * rank] = part
    for n, at in enumerate(range(0, rows, chunk)):
        copies[n].wait()
        for row in range(at, at + chunk, 128):
            total = None
            for k in range(count):
                x = jnp.concatenate(
                    [
                        x_ref[pl.ds(row * span + k, 128, stride=span), :],
                        x_ref[pl.ds(row * span + count + k, 128, stride=span), :],
                    ],
                    axis=1,
                )
                high, middle, low = split3(x)
                wide = w_ref[:, : 2 * rank]
                y = mxu(high, wide) + mxu(middle, wide)
                small = mxu(low, w_ref[:, :rank]) + mxu(high, w_ref[:, 2 * rank :])
                value = y[:, :rank] + y[:, rank:] + small
                p_ref[k, row : row + 128] = value
                term = value * c_ref[k : k + 1, :]
                total = term if total is None else total + term
            b_ref[row : row + 128] = total


def contract(half, x, factor_a, factor_c, rows):
    count, (depth, rank) = factor_c.shape[0], factor_a.shape
    chunk = 256
    return pl.pallas_call(
        functools.partial(contract_kernel, chunk),
        out_shape=[
            jax.ShapeDtypeStruct((count, rows, rank), F32),
            jax.ShapeDtypeStruct((rows, rank), F32),
        ],
        in_specs=[
            pl.BlockSpec(memory_space=pltpu.SMEM),
            pl.BlockSpec(memory_space=pltpu.HBM),
            VMEM,
            VMEM,
        ],
        out_specs=[VMEM, VMEM],
        scratch_shapes=[
            pltpu.VMEM((rows * 2 * count, depth // 2), F32),
            pltpu.VMEM((depth, 3 * rank), BF16),
            pltpu.SemaphoreType.DMA((rows // chunk,)),
        ],
        compiler_params=pltpu.CompilerParams(vmem_limit_bytes=24 << 20),
        name="contract",
    )(half, x, factor_a, factor_c)


def moments_kernel(f_ref, p_ref, c_ref, g_ref):
    f = f_ref[...]
    g_ref[...] = lax.dot_general(
        f, f, (((0,), (0,)), ((), ())), precision=HIGH, preferred_element_type=F32
    )
    for k in range(p_ref.shape[0]):
        c_ref[k : k + 1] = jnp.sum(p_ref[k] * f, axis=0, keepdims=True)


def moments(f, p):
    count, _, rank = p.shape
    return pl.pallas_call(
        moments_kernel,
        out_shape=[
            jax.ShapeDtypeStruct((count, rank), F32),
            jax.ShapeDtypeStruct((rank, rank), F32),
        ],
        in_specs=[VMEM, VMEM],
        out_specs=[VMEM, VMEM],
        compiler_params=pltpu.CompilerParams(vmem_limit_bytes=24 << 20),
        name="moments",
    )(f, p)


def swap(x, axis, bit=1):
    n = lax.axis_size(axis)
    return lax.ppermute(x, axis, [(i, i ^ bit) for i in range(n)])


def gather(x, axes):
    n = lax.axis_size(axes)
    return lax.all_to_all(jnp.broadcast_to(x[None], (n,) + x.shape), axes, 0, 0)


def body(tensor, factor_a, factor_c, gram_c):
    mode_two, mode_three, mode_one = tensor.shape
    rank = factor_a.shape[1]
    core = lax.axis_index("c")
    plane = lax.axis_size(PLANE)
    half = mode_two // 2
    rows = half // plane

    gram_a = dot(factor_a.T, factor_a)
    for axis, bit in (("c", 1), ("xl", 1), ("z", 1), ("z", 2), ("z", 4)):
        gram_a = gram_a + swap(gram_a, axis, bit)
    inverse = inverse_of_product(gram_a, gram_c)

    lanes = mode_one // 2
    flat = tensor.reshape(mode_two, mode_three, 2, lanes).transpose(0, 2, 1, 3)
    flat = flat.reshape(mode_two * mode_three * 2, lanes)
    index = core.astype(jnp.int32).reshape(1)
    p_other, b_other = contract(1 - index, flat, factor_a, factor_c, half)
    p_mine, b_mine = contract(index, flat, factor_a, factor_c, half)
    b_half = b_mine + swap(b_other, "c")
    shares = lax.all_to_all(b_half.reshape(plane, rows, rank), PLANE, 0, 0)
    piece = dot(jnp.sum(shares, axis=0), inverse)

    f_mine = gather(piece, PLANE).reshape(half, rank)
    f_other = swap(f_mine, "c")
    c_mine, g_mine = moments(f_mine, p_mine)
    c_other, g_other = moments(f_other, p_other)
    first = jnp.where(core == 0, f_mine, f_other)
    second = jnp.where(core == 0, f_other, f_mine)
    factor_b = jnp.concatenate([first, second], axis=0)

    local_c = c_mine + c_other
    local_c = local_c + swap(local_c, "c")
    mttkrp_c = jnp.sum(gather(local_c, ("z", "xl", "y")), axis=0)
    lower = jnp.where(core == 0, g_mine, g_other)
    gram_b = lower + jnp.where(core == 0, g_other, g_mine)
    away = [swap(gram_b, "y", bit) for bit in (1, 2, 3)]
    gram_b = (gram_b + away[0]) + (away[1] + away[2])
    factor_c_new = dot(mttkrp_c, inverse_of_product(gram_a, gram_b))
    return (factor_b, factor_c_new)


def solution(mesh):
    axes = (mesh.shape["ia"] // 4, 2, 2, mesh.shape["ja"], mesh.shape["ka"])
    fine = Mesh(mesh.devices.reshape(axes), ("z", "xl", "c", "y", "xh"))
    split = ("z", "xl", "c")
    placed = (P("y", "xh", split), P(split, None), P("xh", None), P())
    return jax.shard_map(
        body, mesh=fine, in_specs=placed, out_specs=(P("y", None), P("xh", None)), check_vma=False
    )
```

```python
import functools

import functools

import jax
import jax.numpy as jnp
from jax import lax
from jax.experimental import pallas as pl
from jax.experimental.pallas import tpu as pltpu
from jax.sharding import Mesh, PartitionSpec as P

HIGH = lax.Precision.HIGHEST
F32 = jnp.float32
BF16 = jnp.bfloat16
PLANE = ("z", "xl", "xh")
VMEM = pl.BlockSpec(memory_space=pltpu.VMEM)


def dot(a, b):
    return jnp.dot(a, b, precision=HIGH, preferred_element_type=F32)


def mxu(a, b):
    return jnp.dot(a, b, preferred_element_type=F32)


def spd_inverse(a, step):
    n = a.shape[0]
    lane = lax.broadcasted_iota(jnp.int32, (step, n), 1)
    row_of = lax.broadcasted_iota(jnp.int32, (step, n), 0)
    lane_all = lax.broadcasted_iota(jnp.int32, (n, n), 1)
    zero = jnp.zeros((step, n), F32)
    for p in range(0, n, step):
        panel = a[p : p + step]
        columns = [jnp.broadcast_to(panel[:, p + c : p + c + 1], (step, n)) for c in range(step)]
        for c in range(step):
            column = columns[c]
            inverse = 1.0 / jnp.broadcast_to(column[c : c + 1], (step, n))
            pivot = row_of == c

            def eliminate(x):
                row = jnp.broadcast_to(x[c : c + 1], (step, n)) * inverse
                return jnp.where(pivot, row, x - column * row)

            panel = eliminate(jnp.where(lane == p + c, jnp.where(pivot, 1.0, 0.0), panel))
            for q in range(c + 1, step):
                columns[q] = eliminate(columns[q])
        spread = [zero] * (p // step) + [panel] + [zero] * ((n - p) // step - 1)
        rest = jnp.where((lane_all >= p) & (lane_all < p + step), 0.0, a)
        rest = rest - dot(a, jnp.concatenate(spread, axis=0))
        pieces = [rest[:p], panel, rest[p + step :]]
        a = jnp.concatenate([x for x in pieces if x.shape[0]], axis=0)
    return a


def inverse_kernel(first_ref, second_ref, out_ref):
    out_ref[...] = spd_inverse(first_ref[...] * second_ref[...], 16)


def inverse_of_product(first, second):
    return pl.pallas_call(
        inverse_kernel,
        out_shape=jax.ShapeDtypeStruct(first.shape, F32),
        in_specs=[VMEM, VMEM],
        out_specs=VMEM,
        cost_estimate=pl.CostEstimate(flops=5 * 10**9, transcendentals=128, bytes_accessed=3 * 2**16),
        name="inverse_of_product",
    )(first, second)


def finish_kernel(first_ref, second_ref, half_ref, mine_hbm, other_hbm, inv_ref, out_hbm, sems):
    half = half_ref[0]
    mine = pltpu.make_async_copy(mine_hbm, out_hbm.at[half], sems.at[0])
    other = pltpu.make_async_copy(other_hbm, out_hbm.at[1 - half], sems.at[1])
    mine.start()
    other.start()
    inv_ref[...] = spd_inverse(first_ref[...] * second_ref[...], 16)
    mine.wait()
    other.wait()


def finish(first, second, half, mine, other):
    anywhere = pl.BlockSpec(memory_space=pl.ANY)
    return pl.pallas_call(
        finish_kernel,
        out_shape=[
            jax.ShapeDtypeStruct(first.shape, F32),
            jax.ShapeDtypeStruct((2,) + mine.shape, F32),
        ],
        in_specs=[VMEM, VMEM, pl.BlockSpec(memory_space=pltpu.SMEM), anywhere, anywhere],
        out_specs=[VMEM, anywhere],
        scratch_shapes=[pltpu.SemaphoreType.DMA((2,))],
        cost_estimate=pl.CostEstimate(flops=5 * 10**9, transcendentals=128, bytes_accessed=2**22),
        name="finish",
    )(first, second, half, mine, other)


def split3(x):
    high = x.astype(BF16)
    rest = x - high.astype(F32)
    middle = rest.astype(BF16)
    return high, middle, (rest - middle.astype(F32)).astype(BF16)


def contract_kernel(chunk, half_ref, x_hbm, a_ref, c_ref, p_ref, b_ref, x_ref, w_ref, sems):
    count, rows, rank = p_ref.shape
    span = 2 * count
    base = half_ref[0] * (rows * span)
    copies = []
    for n, at in enumerate(range(0, rows, chunk)):
        size = chunk * span
        copy = pltpu.make_async_copy(
            x_hbm.at[pl.ds(base + at * span, size)], x_ref.at[pl.ds(at * span, size)], sems.at[n]
        )
        copy.start()
        copies.append(copy)
    for n, part in enumerate(split3(a_ref[...])):
        w_ref[:, n * rank : (n + 1) * rank] = part
    for n, at in enumerate(range(0, rows, chunk)):
        copies[n].wait()
        for row in range(at, at + chunk, 128):
            total = None
            for k in range(count):
                x = jnp.concatenate(
                    [
                        x_ref[pl.ds(row * span + k, 128, stride=span), :],
                        x_ref[pl.ds(row * span + count + k, 128, stride=span), :],
                    ],
                    axis=1,
                )
                high, middle, low = split3(x)
                wide = w_ref[:, : 2 * rank]
                y = mxu(high, wide) + mxu(middle, wide)
                small = mxu(low, w_ref[:, :rank]) + mxu(high, w_ref[:, 2 * rank :])
                value = y[:, :rank] + y[:, rank:] + small
                p_ref[k, row : row + 128] = value
                term = value * c_ref[k : k + 1, :]
                total = term if total is None else total + term
            b_ref[row : row + 128] = total


def contract(half, x, factor_a, factor_c, rows):
    count, (depth, rank) = factor_c.shape[0], factor_a.shape
    chunk = 256
    return pl.pallas_call(
        functools.partial(contract_kernel, chunk),
        out_shape=[
            jax.ShapeDtypeStruct((count, rows, rank), F32),
            jax.ShapeDtypeStruct((rows, rank), F32),
        ],
        in_specs=[
            pl.BlockSpec(memory_space=pltpu.SMEM),
            pl.BlockSpec(memory_space=pltpu.HBM),
            VMEM,
            VMEM,
        ],
        out_specs=[VMEM, VMEM],
        scratch_shapes=[
            pltpu.VMEM((rows * 2 * count, depth // 2), F32),
            pltpu.VMEM((depth, 3 * rank), BF16),
            pltpu.SemaphoreType.DMA((rows // chunk,)),
        ],
        compiler_params=pltpu.CompilerParams(vmem_limit_bytes=24 << 20),
        cost_estimate=pl.CostEstimate(
            flops=16 * count * rows * depth * rank,
            transcendentals=0,
            bytes_accessed=4 * count * rows * (depth + rank),
        ),
        name="contract",
    )(half, x, factor_a, factor_c)


def moments_kernel(f_ref, p_ref, c_ref, g_ref):
    f = f_ref[...]
    g_ref[...] = lax.dot_general(
        f, f, (((0,), (0,)), ((), ())), precision=HIGH, preferred_element_type=F32
    )
    for k in range(p_ref.shape[0]):
        c_ref[k : k + 1] = jnp.sum(p_ref[k] * f, axis=0, keepdims=True)


def moments(f, p):
    count, _, rank = p.shape
    return pl.pallas_call(
        moments_kernel,
        out_shape=[
            jax.ShapeDtypeStruct((count, rank), F32),
            jax.ShapeDtypeStruct((rank, rank), F32),
        ],
        in_specs=[VMEM, VMEM],
        out_specs=[VMEM, VMEM],
        compiler_params=pltpu.CompilerParams(vmem_limit_bytes=24 << 20),
        name="moments",
    )(f, p)


def swap(x, axis, bit=1):
    n = lax.axis_size(axis)
    return lax.ppermute(x, axis, [(i, i ^ bit) for i in range(n)])


def gather(x, axes):
    n = lax.axis_size(axes)
    return lax.all_to_all(jnp.broadcast_to(x[None], (n,) + x.shape), axes, 0, 0)


def body(tensor, factor_a, factor_c, gram_c):
    mode_two, mode_three, mode_one = tensor.shape
    rank = factor_a.shape[1]
    core = lax.axis_index("c")
    plane = lax.axis_size(PLANE)
    half = mode_two // 2
    rows = half // plane
    lanes = mode_one // 2
    flat = tensor.reshape(mode_two, mode_three, 2, lanes).transpose(0, 2, 1, 3)
    flat = flat.reshape(mode_two * mode_three * 2, lanes)
    flat = pltpu.with_memory_space_constraint(flat, pltpu.HBM)
    index = core.astype(jnp.int32).reshape(1)

    gram_a = dot(factor_a.T, factor_a)
    gram_a = gram_a + swap(gram_a, "c")
    other, gram_a = lax.optimization_barrier((1 - index, gram_a))
    p_other, b_other = contract(other, flat, factor_a, factor_c, half)
    gram_a = gram_a + swap(gram_a, "xl")
    index, gram_a = lax.optimization_barrier((index, gram_a))
    p_mine, b_mine = contract(index, flat, factor_a, factor_c, half)
    b_half = b_mine + swap(b_other, "c")
    gram_a = gram_a + swap(gram_a, "z", 1)
    b_half, gram_a = lax.optimization_barrier((b_half, gram_a))
    shares = lax.all_to_all(b_half.reshape(plane, rows, rank), PLANE, 0, 0)
    gram_a = gram_a + swap(gram_a, "z", 2)
    p_other, gram_a = lax.optimization_barrier((p_other, gram_a))
    gram_a = gram_a + swap(gram_a, "z", 4)
    inverse = inverse_of_product(gram_a, gram_c)
    partial = p_mine + swap(p_other, "c")
    shares, partial = lax.optimization_barrier((shares, partial))
    piece = dot(jnp.sum(shares, axis=0), inverse)

    f_mine = gather(piece, PLANE).reshape(half, rank)
    local_c, gram_b = moments(f_mine, partial)
    local_c = local_c + swap(local_c, "c")
    gram_b = gram_b + swap(gram_b, "c")
    away = [swap(gram_b, "y", bit) for bit in (1, 2, 3)]
    mttkrp_c = jnp.sum(gather(local_c, ("z", "xl", "y")), axis=0)
    gram_b = (gram_b + away[0]) + (away[1] + away[2])
    last, factor_b = finish(gram_a, gram_b, index, f_mine, swap(f_mine, "c"))
    factor_b = factor_b.reshape(mode_two, rank)
    factor_c_new = dot(mttkrp_c, last)
    return (factor_b, factor_c_new)


def solution(mesh):
    axes = (mesh.shape["ia"] // 4, 2, 2, mesh.shape["ja"], mesh.shape["ka"])
    fine = Mesh(mesh.devices.reshape(axes), ("z", "xl", "c", "y", "xh"))
    split = ("z", "xl", "c")
    placed = (P("y", "xh", split), P(split, None), P("xh", None), P())
    return jax.shard_map(
        body, mesh=fine, in_specs=placed, out_specs=(P("y", None), P("xh", None)), check_vma=False
    )
```

```python
import functools

import functools

import jax
import jax.numpy as jnp
from jax import lax
from jax.experimental import pallas as pl
from jax.experimental.pallas import tpu as pltpu
from jax.sharding import Mesh, PartitionSpec as P

HIGH = lax.Precision.HIGHEST
F32 = jnp.float32
BF16 = jnp.bfloat16
RING = ("xl", "xh")
VMEM = pl.BlockSpec(memory_space=pltpu.VMEM)
HBM = pl.BlockSpec(memory_space=pltpu.HBM)
SMEM = pl.BlockSpec(memory_space=pltpu.SMEM)


def dot(a, b):
    return jnp.dot(a, b, precision=HIGH, preferred_element_type=F32)


def mxu(a, b):
    return jnp.dot(a, b, preferred_element_type=F32)


def spd_inverse(a, step):
    n = a.shape[0]
    lane = lax.broadcasted_iota(jnp.int32, (step, n), 1)
    row_of = lax.broadcasted_iota(jnp.int32, (step, n), 0)
    lane_all = lax.broadcasted_iota(jnp.int32, (n, n), 1)
    zero = jnp.zeros((step, n), F32)
    for p in range(0, n, step):
        panel = a[p : p + step]
        columns = [jnp.broadcast_to(panel[:, p + c : p + c + 1], (step, n)) for c in range(step)]
        for c in range(step):
            column = columns[c]
            inverse = 1.0 / jnp.broadcast_to(column[c : c + 1], (step, n))
            pivot = row_of == c

            def eliminate(x):
                row = jnp.broadcast_to(x[c : c + 1], (step, n)) * inverse
                return jnp.where(pivot, row, x - column * row)

            panel = eliminate(jnp.where(lane == p + c, jnp.where(pivot, 1.0, 0.0), panel))
            for q in range(c + 1, step):
                columns[q] = eliminate(columns[q])
        spread = [zero] * (p // step) + [panel] + [zero] * ((n - p) // step - 1)
        rest = jnp.where((lane_all >= p) & (lane_all < p + step), 0.0, a)
        rest = rest - dot(a, jnp.concatenate(spread, axis=0))
        pieces = [rest[:p], panel, rest[p + step :]]
        a = jnp.concatenate([x for x in pieces if x.shape[0]], axis=0)
    return a


def inverse_kernel(first_ref, second_ref, out_ref):
    out_ref[...] = spd_inverse(first_ref[...] * second_ref[...], 16)


def inverse_of_product(first, second):
    return pl.pallas_call(
        inverse_kernel,
        out_shape=jax.ShapeDtypeStruct(first.shape, F32),
        in_specs=[VMEM, VMEM],
        out_specs=VMEM,
        cost_estimate=pl.CostEstimate(flops=5 * 10**9, transcendentals=128, bytes_accessed=3 * 2**16),
        name="inverse_of_product",
    )(first, second)


def assemble_kernel(at_ref, mine_ref, other_ref, out_ref):
    count = mine_ref.shape[0]
    for n in range(count):
        out_ref[at_ref[0] * count + (at_ref[1] ^ n)] = mine_ref[n]
        out_ref[(1 - at_ref[0]) * count + (at_ref[1] ^ n)] = other_ref[n]


def assemble(at, mine, other):
    return pl.pallas_call(
        assemble_kernel,
        out_shape=jax.ShapeDtypeStruct((2 * mine.shape[0],) + mine.shape[1:], F32),
        in_specs=[SMEM, VMEM, VMEM],
        out_specs=VMEM,
        name="assemble",
    )(at, mine, other)


def split3(x):
    high = x.astype(BF16)
    rest = x - high.astype(F32)
    middle = rest.astype(BF16)
    return high, middle, (rest - middle.astype(F32)).astype(BF16)


def contract_kernel(chunk, at_ref, x_hbm, a_ref, c_ref, p_hbm, b_ref, x_ref, w_ref, p_ref, sems):
    count, rows, rank = p_ref.shape
    span = 2 * count
    copies = []
    for n, at in enumerate(range(0, rows, chunk)):
        size = chunk * span
        block = at_ref[0] * (rows // chunk) + (at_ref[1] ^ n)
        copy = pltpu.make_async_copy(
            x_hbm.at[pl.ds(block * size, size)], x_ref.at[pl.ds(at * span, size)], sems.at[n]
        )
        copy.start()
        copies.append(copy)
    for n, part in enumerate(split3(a_ref[...])):
        w_ref[:, n * rank : (n + 1) * rank] = part
    for n, at in enumerate(range(0, rows, chunk)):
        copies[n].wait()
        for row in range(at, at + chunk, 128):
            total = None
            for k in range(count):
                x = jnp.concatenate(
                    [
                        x_ref[pl.ds(row * span + k, 128, stride=span), :],
                        x_ref[pl.ds(row * span + count + k, 128, stride=span), :],
                    ],
                    axis=1,
                )
                high, middle, low = split3(x)
                wide = w_ref[:, : 2 * rank]
                y = mxu(high, wide) + mxu(middle, wide)
                small = mxu(low, w_ref[:, :rank]) + mxu(high, w_ref[:, 2 * rank :])
                value = y[:, :rank] + y[:, rank:] + small
                p_ref[k, row : row + 128] = value
                term = value * c_ref[k : k + 1, :]
                total = term if total is None else total + term
            b_ref[row : row + 128] = total
        copy = pltpu.make_async_copy(
            p_ref.at[:, pl.ds(at, chunk)],
            p_hbm.at[:, pl.ds(at, chunk)],
            sems.at[len(copies)],
        )
        copy.start()
        copies.append(copy)
    for copy in copies[rows // chunk :]:
        copy.wait()


def contract(at, x, factor_a, factor_c, rows):
    count, (depth, rank) = factor_c.shape[0], factor_a.shape
    chunk = rows // 4
    return pl.pallas_call(
        functools.partial(contract_kernel, chunk),
        out_shape=[
            pltpu.HBM((count, rows, rank), F32),
            jax.ShapeDtypeStruct((rows, rank), F32),
        ],
        in_specs=[SMEM, HBM, VMEM, VMEM],
        out_specs=[HBM, VMEM],
        scratch_shapes=[
            pltpu.VMEM((rows * 2 * count, depth // 2), F32),
            pltpu.VMEM((depth, 3 * rank), BF16),
            pltpu.VMEM((count, rows, rank), F32),
            pltpu.SemaphoreType.DMA((2 * rows // chunk,)),
        ],
        compiler_params=pltpu.CompilerParams(vmem_limit_bytes=24 << 20),
        cost_estimate=pl.CostEstimate(
            flops=16 * count * rows * depth * rank,
            transcendentals=0,
            bytes_accessed=4 * count * rows * (depth + rank),
        ),
        name="contract",
    )(at, x, factor_a, factor_c)


def parcels_kernel(x_ref, b_ref, b_far_ref, g_ref, g_far_ref, *outs):
    depth, rows, _ = outs[0].shape
    block, slab = b_ref.shape[0] // 4, g_ref.shape[0] // 4
    some, few = block // depth, slab // depth
    for n, out in enumerate(outs):
        for z in range(depth):
            at = n * block + z * some
            out[z, :some] = b_ref[at : at + some] + b_far_ref[at : at + some]
        for a in range(4):

            @pl.when((x_ref[0] ^ n) == a)
            def _():
                for z in range(depth):
                    at = a * slab + z * few
                    out[z, some:] = 0.5 * (g_ref[at : at + few] + g_far_ref[at : at + few])


def parcels(x, b, b_far, g, g_far, depth):
    rank = b.shape[1]
    shape = jax.ShapeDtypeStruct((depth, (b.shape[0] + g.shape[0]) // (4 * depth), rank), F32)
    return pl.pallas_call(
        parcels_kernel,
        out_shape=[shape] * 4,
        in_specs=[SMEM] + [VMEM] * 4,
        out_specs=[VMEM] * 4,
        name="parcels",
    )(x, b, b_far, g, g_far)


def spread_kernel(x_ref, out_ref):
    out_ref[...] = jnp.broadcast_to(jnp.sum(x_ref[...], axis=0)[None], out_ref.shape)


def spread(x):
    return pl.pallas_call(
        spread_kernel,
        out_shape=jax.ShapeDtypeStruct(x.shape, F32),
        in_specs=[VMEM],
        out_specs=VMEM,
        name="spread",
    )(x)


def solve_kernel(x_ref, *refs):
    columns, (h_ref, p_hbm, q_hbm, g_ref, f_ref, out_ref, p_ref, q_ref, sems) = refs[:4], refs[4:]
    depth, every, rank = columns[0].shape
    few = rank // (4 * depth)
    some = every - few
    copies = [
        pltpu.make_async_copy(p_hbm, p_ref, sems.at[0]),
        pltpu.make_async_copy(q_hbm, q_ref, sems.at[1]),
    ]
    for copy in copies:
        copy.start()
    for n in range(4):
        for a in range(4):

            @pl.when((x_ref[0] ^ n) == a)
            def _():
                for z in range(depth):
                    at = (a * depth + z) * few
                    g_ref[at : at + few] = columns[n][z, some:]

    inverse = spd_inverse(g_ref[...] * h_ref[...], 16)
    block = depth * some
    for n in range(4):
        f = dot(columns[n][:, :some].reshape(block, rank), inverse)
        f_ref[n * block : (n + 1) * block] = f
    f = f_ref[...]
    out_ref[:rank] = lax.dot_general(
        f, f, (((0,), (0,)), ((), ())), precision=HIGH, preferred_element_type=F32
    )
    out_ref[rank:] = jnp.zeros((out_ref.shape[0] - rank, rank), F32)
    for copy in copies:
        copy.wait()
    for k in range(p_ref.shape[0]):
        both = (p_ref[k] + q_ref[k]) * f_ref[...]
        out_ref[rank + k : rank + k + 1] = jnp.sum(both, axis=0, keepdims=True)


def solve(x, columns, gram_c, first, second):
    count, rows, rank = first.shape
    square = jax.ShapeDtypeStruct((rank, rank), F32)
    return pl.pallas_call(
        solve_kernel,
        out_shape=[
            square,
            jax.ShapeDtypeStruct((rows, rank), F32),
            jax.ShapeDtypeStruct((rank + 8 * pl.cdiv(count, 8), rank), F32),
        ],
        in_specs=[SMEM] + [VMEM] * 5 + [HBM] * 2,
        out_specs=[VMEM] * 3,
        scratch_shapes=[
            pltpu.VMEM((count, rows, rank), F32),
            pltpu.VMEM((count, rows, rank), F32),
            pltpu.SemaphoreType.DMA((2,)),
        ],
        compiler_params=pltpu.CompilerParams(vmem_limit_bytes=24 << 20),
        name="solve",
    )(x, *columns, gram_c, first, second)


def swap(x, axis, bit=1):
    n = lax.axis_size(axis)
    return lax.ppermute(x, axis, [(i, i ^ bit) for i in range(n)])


def gather(x, axes):
    n = lax.axis_size(axes)
    return lax.all_to_all(jnp.broadcast_to(x[None], (n,) + x.shape), axes, 0, 0)


def body(tensor, factor_a, factor_c, gram_c):
    mode_two, mode_three, mode_one = tensor.shape
    rank = factor_a.shape[1]
    core = lax.axis_index("c").astype(jnp.int32)
    x = lax.axis_index(RING).astype(jnp.int32)
    depth = lax.axis_size("z")
    half = mode_two // 2
    lanes = mode_one // 2
    flat = tensor.reshape(mode_two, mode_three, 2, lanes).transpose(0, 2, 1, 3)
    flat = flat.reshape(mode_two * mode_three * 2, lanes)
    flat = pltpu.with_memory_space_constraint(flat, pltpu.HBM)

    p_other, b_other = contract(jnp.stack([1 - core, x]), flat, factor_a, factor_c, half)
    p_mine, b_mine = contract(jnp.stack([core, x]), flat, factor_a, factor_c, half)
    gram_part = dot(factor_a.T, factor_a)
    at = x.reshape(1)
    sent = parcels(at, b_mine, swap(b_other, "c"), gram_part, swap(gram_part, "c"), depth)
    got = [sent[0]] + [swap(sent[n], RING, n) for n in (1, 2, 3)]
    column = (got[0] + got[1]) + (got[2] + got[3])
    column = spread(lax.all_to_all(column, "z", 0, 0))
    column = lax.all_to_all(column, "z", 0, 0)
    columns = [column] + [swap(column, RING, n) for n in (1, 2, 3)]
    gram_a, f_mine, sums = solve(at, columns, gram_c, p_mine, swap(p_other, "c"))

    sums = sums + swap(sums, "c")
    away = [swap(sums, "y", bit) for bit in (1, 2, 3)]
    sums = (sums + away[0]) + (away[1] + away[2])
    gram_b, local_c = sums[:rank], sums[rank : rank + mode_three]
    mttkrp_c = jnp.sum(gather(local_c, ("z", "xl")), axis=0)
    last, f_other = lax.optimization_barrier(
        (inverse_of_product(gram_a, gram_b), swap(f_mine, "c"))
    )
    shape = (4, half // 4, rank)
    factor_b = assemble(jnp.stack([core, x]), f_mine.reshape(shape), f_other.reshape(shape))
    factor_c_new = dot(mttkrp_c, last)
    return (factor_b.reshape(mode_two, rank), factor_c_new)


def solution(mesh):
    axes = (mesh.shape["ia"] // 4, 2, 2, mesh.shape["ja"], mesh.shape["ka"])
    fine = Mesh(mesh.devices.reshape(axes), ("z", "xl", "c", "y", "xh"))
    split = ("z", "xl", "c")
    placed = (P("y", "xh", split), P(split, None), P("xh", None), P())
    return jax.shard_map(
        body, mesh=fine, in_specs=placed, out_specs=(P("y", None), P("xh", None)), check_vma=False
    )
```

```python
import functools

import functools

import jax
import jax.numpy as jnp
from jax import lax
from jax.experimental import pallas as pl
from jax.experimental.pallas import tpu as pltpu
from jax.sharding import Mesh, PartitionSpec as P

HIGH = lax.Precision.HIGHEST
F32 = jnp.float32
BF16 = jnp.bfloat16
RING = ("xl", "xh")
VMEM = pl.BlockSpec(memory_space=pltpu.VMEM)
HBM = pl.BlockSpec(memory_space=pltpu.HBM)
SMEM = pl.BlockSpec(memory_space=pltpu.SMEM)


def dot(a, b):
    return jnp.dot(a, b, precision=HIGH, preferred_element_type=F32)


def mxu(a, b):
    return jnp.dot(a, b, preferred_element_type=F32)


def spd_inverse(a, step):
    n = a.shape[0]
    lane = lax.broadcasted_iota(jnp.int32, (step, n), 1)
    row_of = lax.broadcasted_iota(jnp.int32, (step, n), 0)
    lane_all = lax.broadcasted_iota(jnp.int32, (n, n), 1)
    zero = jnp.zeros((step, n), F32)
    for p in range(0, n, step):
        panel = a[p : p + step]
        columns = [jnp.broadcast_to(panel[:, p + c : p + c + 1], (step, n)) for c in range(step)]
        for c in range(step):
            column = columns[c]
            inverse = 1.0 / jnp.broadcast_to(column[c : c + 1], (step, n))
            pivot = row_of == c

            def eliminate(x):
                row = jnp.broadcast_to(x[c : c + 1], (step, n)) * inverse
                return jnp.where(pivot, row, x - column * row)

            panel = eliminate(jnp.where(lane == p + c, jnp.where(pivot, 1.0, 0.0), panel))
            for q in range(c + 1, step):
                columns[q] = eliminate(columns[q])
        spread = [zero] * (p // step) + [panel] + [zero] * ((n - p) // step - 1)
        rest = jnp.where((lane_all >= p) & (lane_all < p + step), 0.0, a)
        rest = rest - dot(a, jnp.concatenate(spread, axis=0))
        pieces = [rest[:p], panel, rest[p + step :]]
        a = jnp.concatenate([x for x in pieces if x.shape[0]], axis=0)
    return a


def total(refs, rows):
    first, second, third, fourth = (ref[rows] for ref in refs)
    return (first + second) + (third + fourth)


def collect_kernel(*refs):
    out_ref = refs[-1]
    count, rank = out_ref.shape[1:]
    part = total(refs[:-1], pl.ds(rank, count))
    out_ref[...] = jnp.broadcast_to(part[None], out_ref.shape)


def collect(parts, copies, count):
    rank = parts[0].shape[1]
    return pl.pallas_call(
        collect_kernel,
        out_shape=jax.ShapeDtypeStruct((copies, count, rank), F32),
        in_specs=[VMEM] * 4,
        out_specs=VMEM,
        compiler_params=pltpu.CompilerParams(vmem_limit_bytes=2 << 20),
        name="collect",
    )(*parts)


def inverse_kernel(first_ref, *refs):
    out_ref = refs[-1]
    second = total(refs[:-1], pl.ds(0, first_ref.shape[0]))
    out_ref[...] = spd_inverse(first_ref[...] * second, 16)


def inverse_of_product(first, parts):
    return pl.pallas_call(
        inverse_kernel,
        out_shape=jax.ShapeDtypeStruct(first.shape, F32),
        in_specs=[VMEM] * 5,
        out_specs=VMEM,
        compiler_params=pltpu.CompilerParams(vmem_limit_bytes=4 << 20),
        name="inverse_of_product",
    )(first, *parts)


def assemble_kernel(at_ref, mine_ref, other_ref, out_ref):
    count = mine_ref.shape[0]
    for n in range(count):
        out_ref[at_ref[0] * count + (at_ref[1] ^ n)] = mine_ref[n]
        out_ref[(1 - at_ref[0]) * count + (at_ref[1] ^ n)] = other_ref[n]


def assemble(at, mine, other):
    return pl.pallas_call(
        assemble_kernel,
        out_shape=jax.ShapeDtypeStruct((2 * mine.shape[0],) + mine.shape[1:], F32),
        in_specs=[SMEM, VMEM, VMEM],
        out_specs=VMEM,
        compiler_params=pltpu.CompilerParams(vmem_limit_bytes=8 << 20),
        name="assemble",
    )(at, mine, other)


def split3(x):
    high = x.astype(BF16)
    rest = x - high.astype(F32)
    middle = rest.astype(BF16)
    return high, middle, (rest - middle.astype(F32)).astype(BF16)


def contract_kernel(chunk, at_ref, x_hbm, a_hbm, c_hbm, p_hbm, b_ref, *scratch):
    x_ref, w_ref, p_ref, a_ref, c_ref, sems = scratch
    count, rows, rank = p_ref.shape
    span = 2 * count
    factors = [
        pltpu.make_async_copy(a_hbm, a_ref, sems.at[2 * rows // chunk]),
        pltpu.make_async_copy(c_hbm, c_ref, sems.at[2 * rows // chunk + 1]),
    ]
    factors[0].start()
    factors[1].start()
    copies = []
    for n, at in enumerate(range(0, rows, chunk)):
        size = chunk * span
        block = at_ref[0] * (rows // chunk) + (at_ref[1] ^ n)
        copy = pltpu.make_async_copy(
            x_hbm.at[pl.ds(block * size, size)], x_ref.at[pl.ds(at * span, size)], sems.at[n]
        )
        copy.start()
        copies.append(copy)
    factors[0].wait()
    factors[1].wait()
    for n, part in enumerate(split3(a_ref[...])):
        w_ref[:, n * rank : (n + 1) * rank] = part
    for n, at in enumerate(range(0, rows, chunk)):
        copies[n].wait()
        for row in range(at, at + chunk, 128):
            total = None
            for k in range(count):
                x = jnp.concatenate(
                    [
                        x_ref[pl.ds(row * span + k, 128, stride=span), :],
                        x_ref[pl.ds(row * span + count + k, 128, stride=span), :],
                    ],
                    axis=1,
                )
                high, middle, low = split3(x)
                wide = w_ref[:, : 2 * rank]
                y = mxu(high, wide) + mxu(middle, wide)
                small = mxu(low, w_ref[:, :rank]) + mxu(high, w_ref[:, 2 * rank :])
                value = y[:, :rank] + y[:, rank:] + small
                p_ref[k, row : row + 128] = value
                term = value * c_ref[k : k + 1, :]
                total = term if total is None else total + term
            b_ref[row : row + 128] = total
        copy = pltpu.make_async_copy(
            p_ref.at[:, pl.ds(at, chunk)],
            p_hbm.at[:, pl.ds(at, chunk)],
            sems.at[len(copies)],
        )
        copy.start()
        copies.append(copy)
    for copy in copies[rows // chunk :]:
        copy.wait()


def contract(at, x, factor_a, factor_c, rows):
    count, (depth, rank) = factor_c.shape[0], factor_a.shape
    chunk = rows // 4
    return pl.pallas_call(
        functools.partial(contract_kernel, chunk),
        out_shape=[
            pltpu.HBM((count, rows, rank), F32),
            jax.ShapeDtypeStruct((rows, rank), F32),
        ],
        in_specs=[SMEM, HBM, HBM, HBM],
        out_specs=[HBM, VMEM],
        scratch_shapes=[
            pltpu.VMEM((rows * 2 * count, depth // 2), F32),
            pltpu.VMEM((depth, 3 * rank), BF16),
            pltpu.VMEM((count, rows, rank), F32),
            pltpu.VMEM((depth, rank), F32),
            pltpu.VMEM((count, rank), F32),
            pltpu.SemaphoreType.DMA((2 * rows // chunk + 2,)),
        ],
        compiler_params=pltpu.CompilerParams(vmem_limit_bytes=12 << 20),
        cost_estimate=pl.CostEstimate(
            flops=16 * count * rows * depth * rank,
            transcendentals=0,
            bytes_accessed=4 * count * rows * (depth + rank),
        ),
        name="contract",
    )(at, x, factor_a, factor_c)


def parcels_kernel(x_ref, b_ref, b_far_ref, g_ref, g_far_ref, *outs):
    depth, rows, _ = outs[0].shape
    block, slab = b_ref.shape[0] // 4, g_ref.shape[0] // 4
    some, few = block // depth, slab // depth
    for n, out in enumerate(outs):
        for z in range(depth):
            at = n * block + z * some
            out[z, :some] = b_ref[at : at + some] + b_far_ref[at : at + some]
        for a in range(4):

            @pl.when((x_ref[0] ^ n) == a)
            def _():
                for z in range(depth):
                    at = a * slab + z * few
                    out[z, some:] = 0.5 * (g_ref[at : at + few] + g_far_ref[at : at + few])


def parcels(x, b, b_far, g, g_far, depth):
    rank = b.shape[1]
    shape = jax.ShapeDtypeStruct((depth, (b.shape[0] + g.shape[0]) // (4 * depth), rank), F32)
    return pl.pallas_call(
        parcels_kernel,
        out_shape=[shape] * 4,
        in_specs=[SMEM] + [VMEM] * 4,
        out_specs=[VMEM] * 4,
        compiler_params=pltpu.CompilerParams(vmem_limit_bytes=6 << 20),
        name="parcels",
    )(x, b, b_far, g, g_far)


def spread_kernel(x_ref, out_ref):
    out_ref[...] = jnp.broadcast_to(jnp.sum(x_ref[...], axis=0)[None], out_ref.shape)


def spread(x):
    return pl.pallas_call(
        spread_kernel,
        out_shape=jax.ShapeDtypeStruct(x.shape, F32),
        in_specs=[VMEM],
        out_specs=VMEM,
        compiler_params=pltpu.CompilerParams(vmem_limit_bytes=2 << 20),
        name="spread",
    )(x)


def solve_kernel(x_ref, *refs):
    columns, (h_ref, p_hbm, q_hbm, g_ref, f_ref, out_ref, p_ref, q_ref, sems) = refs[:4], refs[4:]
    depth, every, rank = columns[0].shape
    few = rank // (4 * depth)
    some = every - few
    copies = [
        pltpu.make_async_copy(p_hbm, p_ref, sems.at[0]),
        pltpu.make_async_copy(q_hbm, q_ref, sems.at[1]),
    ]
    for copy in copies:
        copy.start()
    for n in range(4):
        for a in range(4):

            @pl.when((x_ref[0] ^ n) == a)
            def _():
                for z in range(depth):
                    at = (a * depth + z) * few
                    g_ref[at : at + few] = columns[n][z, some:]

    inverse = spd_inverse(g_ref[...] * h_ref[...], 16)
    block = depth * some
    for n in range(4):
        f = dot(columns[n][:, :some].reshape(block, rank), inverse)
        f_ref[n * block : (n + 1) * block] = f
    f = f_ref[...]
    out_ref[:rank] = lax.dot_general(
        f, f, (((0,), (0,)), ((), ())), precision=HIGH, preferred_element_type=F32
    )
    out_ref[rank:] = jnp.zeros((out_ref.shape[0] - rank, rank), F32)
    for copy in copies:
        copy.wait()
    for k in range(p_ref.shape[0]):
        both = (p_ref[k] + q_ref[k]) * f_ref[...]
        out_ref[rank + k : rank + k + 1] = jnp.sum(both, axis=0, keepdims=True)


def solve(x, columns, gram_c, first, second):
    count, rows, rank = first.shape
    square = jax.ShapeDtypeStruct((rank, rank), F32)
    return pl.pallas_call(
        solve_kernel,
        out_shape=[
            square,
            jax.ShapeDtypeStruct((rows, rank), F32),
            jax.ShapeDtypeStruct((rank + 8 * pl.cdiv(count, 8), rank), F32),
        ],
        in_specs=[SMEM] + [VMEM] * 5 + [HBM] * 2,
        out_specs=[VMEM] * 3,
        scratch_shapes=[
            pltpu.VMEM((count, rows, rank), F32),
            pltpu.VMEM((count, rows, rank), F32),
            pltpu.SemaphoreType.DMA((2,)),
        ],
        compiler_params=pltpu.CompilerParams(vmem_limit_bytes=12 << 20),
        name="solve",
    )(x, *columns, gram_c, first, second)


def swap(x, axis, bit=1):
    n = lax.axis_size(axis)
    return lax.ppermute(x, axis, [(i, i ^ bit) for i in range(n)])


def body(tensor, factor_a, factor_c, gram_c):
    mode_two, mode_three, mode_one = tensor.shape
    rank = factor_a.shape[1]
    core = lax.axis_index("c").astype(jnp.int32)
    x = lax.axis_index(RING).astype(jnp.int32)
    depth = lax.axis_size("z")
    half = mode_two // 2
    lanes = mode_one // 2
    flat = tensor.reshape(mode_two, mode_three, 2, lanes).transpose(0, 2, 1, 3)
    flat = flat.reshape(mode_two * mode_three * 2, lanes)
    flat, a_hbm, c_hbm = (
        pltpu.with_memory_space_constraint(v, pltpu.HBM) for v in (flat, factor_a, factor_c)
    )

    p_other, b_other = contract(jnp.stack([1 - core, x]), flat, a_hbm, c_hbm, half)
    p_mine, b_mine = contract(jnp.stack([core, x]), flat, a_hbm, c_hbm, half)
    gram_part = dot(factor_a.T, factor_a)
    at = x.reshape(1)
    sent = parcels(at, b_mine, swap(b_other, "c"), gram_part, swap(gram_part, "c"), depth)
    got = [sent[0]] + [swap(sent[n], RING, n) for n in (1, 2, 3)]
    column = (got[0] + got[1]) + (got[2] + got[3])
    column = spread(lax.all_to_all(column, "z", 0, 0))
    column = lax.all_to_all(column, "z", 0, 0)
    columns = [column] + [swap(column, RING, n) for n in (1, 2, 3)]
    gram_a, f_mine, sums = solve(at, columns, gram_c, p_mine, swap(p_other, "c"))

    sums = sums + swap(sums, "c")
    parts = [sums] + [swap(sums, "y", bit) for bit in (1, 2, 3)]
    plane = ("z", "xl")
    spread_c = collect(parts, lax.axis_size(plane), mode_three)
    spread_c, f_mine = lax.optimization_barrier((spread_c, f_mine))
    mttkrp_c = jnp.sum(lax.all_to_all(spread_c, plane, 0, 0), axis=0)
    f_other = swap(f_mine, "c")
    shape = (4, half // 4, rank)
    factor_b = assemble(jnp.stack([core, x]), f_mine.reshape(shape), f_other.reshape(shape))
    gram_a, factor_b = lax.optimization_barrier((gram_a, factor_b))
    factor_c_new = dot(mttkrp_c, inverse_of_product(gram_a, parts))
    return (factor_b.reshape(mode_two, rank), factor_c_new)


def solution(mesh):
    axes = (mesh.shape["ia"] // 4, 2, 2, mesh.shape["ja"], mesh.shape["ka"])
    fine = Mesh(mesh.devices.reshape(axes), ("z", "xl", "c", "y", "xh"))
    split = ("z", "xl", "c")
    placed = (P("y", "xh", split), P(split, None), P("xh", None), P())
    return jax.shard_map(
        body, mesh=fine, in_specs=placed, out_specs=(P("y", None), P("xh", None)), check_vma=False
    )
```

```python
import functools

import functools

import jax
import jax.numpy as jnp
from jax import lax
from jax.experimental import pallas as pl
from jax.experimental.pallas import tpu as pltpu
from jax.sharding import Mesh, PartitionSpec as P

HIGH = lax.Precision.HIGHEST
F32 = jnp.float32
BF16 = jnp.bfloat16
RING = ("xl", "xh")
VMEM = pl.BlockSpec(memory_space=pltpu.VMEM)
HBM = pl.BlockSpec(memory_space=pltpu.HBM)
SMEM = pl.BlockSpec(memory_space=pltpu.SMEM)


def dot(a, b):
    return jnp.dot(a, b, precision=HIGH, preferred_element_type=F32)


def mxu(a, b):
    return jnp.dot(a, b, preferred_element_type=F32)


def spd_inverse(a, step):
    n = a.shape[0]
    lane = lax.broadcasted_iota(jnp.int32, (step, n), 1)
    row_of = lax.broadcasted_iota(jnp.int32, (step, n), 0)
    lane_all = lax.broadcasted_iota(jnp.int32, (n, n), 1)
    zero = jnp.zeros((step, n), F32)
    for p in range(0, n, step):
        panel = a[p : p + step]
        columns = [jnp.broadcast_to(panel[:, p + c : p + c + 1], (step, n)) for c in range(step)]
        for c in range(step):
            column = columns[c]
            inverse = 1.0 / jnp.broadcast_to(column[c : c + 1], (step, n))
            pivot = row_of == c

            def eliminate(x):
                row = jnp.broadcast_to(x[c : c + 1], (step, n)) * inverse
                return jnp.where(pivot, row, x - column * row)

            panel = eliminate(jnp.where(lane == p + c, jnp.where(pivot, 1.0, 0.0), panel))
            for q in range(c + 1, step):
                columns[q] = eliminate(columns[q])
        spread = [zero] * (p // step) + [panel] + [zero] * ((n - p) // step - 1)
        rest = jnp.where((lane_all >= p) & (lane_all < p + step), 0.0, a)
        rest = rest - dot(a, jnp.concatenate(spread, axis=0))
        pieces = [rest[:p], panel, rest[p + step :]]
        a = jnp.concatenate([x for x in pieces if x.shape[0]], axis=0)
    return a


def total(refs, rows):
    first, second, third, fourth = (ref[rows] for ref in refs)
    return (first + second) + (third + fourth)


def collect_kernel(*refs):
    out_ref = refs[-1]
    count, rank = out_ref.shape[1:]
    part = total(refs[:-1], pl.ds(rank, count))
    out_ref[...] = jnp.broadcast_to(part[None], out_ref.shape)


def collect(parts, copies, count):
    rank = parts[0].shape[1]
    return pl.pallas_call(
        collect_kernel,
        out_shape=jax.ShapeDtypeStruct((copies, count, rank), F32),
        in_specs=[VMEM] * 4,
        out_specs=VMEM,
        compiler_params=pltpu.CompilerParams(vmem_limit_bytes=2 << 20),
        name="collect",
    )(*parts)


def inverse_kernel(first_ref, *refs):
    out_ref = refs[-1]
    second = total(refs[:-1], pl.ds(0, first_ref.shape[0]))
    out_ref[...] = spd_inverse(first_ref[...] * second, 16)


def inverse_of_product(first, parts):
    return pl.pallas_call(
        inverse_kernel,
        out_shape=jax.ShapeDtypeStruct(first.shape, F32),
        in_specs=[VMEM] * 5,
        out_specs=VMEM,
        compiler_params=pltpu.CompilerParams(vmem_limit_bytes=4 << 20),
        cost_estimate=pl.CostEstimate(flops=3 * 10**9, transcendentals=128, bytes_accessed=2**19),
        name="inverse_of_product",
    )(first, *parts)


def assemble_kernel(at_ref, mine_ref, other_ref, out_ref):
    count = mine_ref.shape[0]
    for n in range(count):
        out_ref[at_ref[0] * count + (at_ref[1] ^ n)] = mine_ref[n]
        out_ref[(1 - at_ref[0]) * count + (at_ref[1] ^ n)] = other_ref[n]


def assemble(at, mine, other):
    return pl.pallas_call(
        assemble_kernel,
        out_shape=jax.ShapeDtypeStruct((2 * mine.shape[0],) + mine.shape[1:], F32),
        in_specs=[SMEM, VMEM, VMEM],
        out_specs=VMEM,
        compiler_params=pltpu.CompilerParams(vmem_limit_bytes=8 << 20),
        name="assemble",
    )(at, mine, other)


def split3(x):
    high = x.astype(BF16)
    rest = x - high.astype(F32)
    middle = rest.astype(BF16)
    return high, middle, (rest - middle.astype(F32)).astype(BF16)


def contract_kernel(chunk, at_ref, x_hbm, a_hbm, c_hbm, p_hbm, b_ref, *scratch):
    x_ref, w_ref, p_ref, a_ref, c_ref, sems = scratch
    count, rows, rank = p_ref.shape
    span = 2 * count
    factors = [
        pltpu.make_async_copy(a_hbm, a_ref, sems.at[2 * rows // chunk]),
        pltpu.make_async_copy(c_hbm, c_ref, sems.at[2 * rows // chunk + 1]),
    ]
    factors[0].start()
    factors[1].start()
    copies = []
    for n, at in enumerate(range(0, rows, chunk)):
        size = chunk * span
        block = at_ref[0] * (rows // chunk) + (at_ref[1] ^ n)
        copy = pltpu.make_async_copy(
            x_hbm.at[pl.ds(block * size, size)], x_ref.at[pl.ds(at * span, size)], sems.at[n]
        )
        copy.start()
        copies.append(copy)
    factors[0].wait()
    factors[1].wait()
    for n, part in enumerate(split3(a_ref[...])):
        w_ref[:, n * rank : (n + 1) * rank] = part
    for n, at in enumerate(range(0, rows, chunk)):
        copies[n].wait()
        for row in range(at, at + chunk, 128):
            total = None
            for k in range(count):
                x = jnp.concatenate(
                    [
                        x_ref[pl.ds(row * span + k, 128, stride=span), :],
                        x_ref[pl.ds(row * span + count + k, 128, stride=span), :],
                    ],
                    axis=1,
                )
                high, middle, low = split3(x)
                wide = w_ref[:, : 2 * rank]
                y = mxu(high, wide) + mxu(middle, wide)
                small = mxu(low, w_ref[:, :rank]) + mxu(high, w_ref[:, 2 * rank :])
                value = y[:, :rank] + y[:, rank:] + small
                p_ref[k, row : row + 128] = value
                term = value * c_ref[k : k + 1, :]
                total = term if total is None else total + term
            b_ref[row : row + 128] = total
        copy = pltpu.make_async_copy(
            p_ref.at[:, pl.ds(at, chunk)],
            p_hbm.at[:, pl.ds(at, chunk)],
            sems.at[len(copies)],
        )
        copy.start()
        copies.append(copy)
    for copy in copies[rows // chunk :]:
        copy.wait()


def contract(at, x, factor_a, factor_c, rows):
    count, (depth, rank) = factor_c.shape[0], factor_a.shape
    chunk = rows // 4
    return pl.pallas_call(
        functools.partial(contract_kernel, chunk),
        out_shape=[
            pltpu.HBM((count, rows, rank), F32),
            jax.ShapeDtypeStruct((rows, rank), F32),
        ],
        in_specs=[SMEM, HBM, HBM, HBM],
        out_specs=[HBM, VMEM],
        scratch_shapes=[
            pltpu.VMEM((rows * 2 * count, depth // 2), F32),
            pltpu.VMEM((depth, 3 * rank), BF16),
            pltpu.VMEM((count, rows, rank), F32),
            pltpu.VMEM((depth, rank), F32),
            pltpu.VMEM((count, rank), F32),
            pltpu.SemaphoreType.DMA((2 * rows // chunk + 2,)),
        ],
        compiler_params=pltpu.CompilerParams(vmem_limit_bytes=12 << 20),
        cost_estimate=pl.CostEstimate(
            flops=16 * count * rows * depth * rank,
            transcendentals=0,
            bytes_accessed=4 * count * rows * (depth + rank),
        ),
        name="contract",
    )(at, x, factor_a, factor_c)


def parcels_kernel(x_ref, b_ref, b_far_ref, g_ref, g_far_ref, *outs):
    depth, rows, _ = outs[0].shape
    block, slab = b_ref.shape[0] // 4, g_ref.shape[0] // 4
    some, few = block // depth, slab // depth
    for n, out in enumerate(outs):
        for z in range(depth):
            at = n * block + z * some
            out[z, :some] = b_ref[at : at + some] + b_far_ref[at : at + some]
        for a in range(4):

            @pl.when((x_ref[0] ^ n) == a)
            def _():
                for z in range(depth):
                    at = a * slab + z * few
                    out[z, some:] = 0.5 * (g_ref[at : at + few] + g_far_ref[at : at + few])


def parcels(x, b, b_far, g, g_far, depth):
    rank = b.shape[1]
    shape = jax.ShapeDtypeStruct((depth, (b.shape[0] + g.shape[0]) // (4 * depth), rank), F32)
    return pl.pallas_call(
        parcels_kernel,
        out_shape=[shape] * 4,
        in_specs=[SMEM] + [VMEM] * 4,
        out_specs=[VMEM] * 4,
        compiler_params=pltpu.CompilerParams(vmem_limit_bytes=6 << 20),
        name="parcels",
    )(x, b, b_far, g, g_far)


def spread_kernel(x_ref, out_ref):
    out_ref[...] = jnp.broadcast_to(jnp.sum(x_ref[...], axis=0)[None], out_ref.shape)


def spread(x):
    return pl.pallas_call(
        spread_kernel,
        out_shape=jax.ShapeDtypeStruct(x.shape, F32),
        in_specs=[VMEM],
        out_specs=VMEM,
        compiler_params=pltpu.CompilerParams(vmem_limit_bytes=2 << 20),
        name="spread",
    )(x)


def solve_kernel(x_ref, *refs):
    columns, (h_ref, p_hbm, q_hbm, g_ref, f_ref, out_ref, p_ref, q_ref, sems) = refs[:4], refs[4:]
    depth, every, rank = columns[0].shape
    few = rank // (4 * depth)
    some = every - few
    copies = [
        pltpu.make_async_copy(p_hbm, p_ref, sems.at[0]),
        pltpu.make_async_copy(q_hbm, q_ref, sems.at[1]),
    ]
    for copy in copies:
        copy.start()
    for n in range(4):
        for a in range(4):

            @pl.when((x_ref[0] ^ n) == a)
            def _():
                for z in range(depth):
                    at = (a * depth + z) * few
                    g_ref[at : at + few] = columns[n][z, some:]

    inverse = spd_inverse(g_ref[...] * h_ref[...], 16)
    block = depth * some
    for n in range(4):
        f = dot(columns[n][:, :some].reshape(block, rank), inverse)
        f_ref[n * block : (n + 1) * block] = f
    f = f_ref[...]
    out_ref[:rank] = lax.dot_general(
        f, f, (((0,), (0,)), ((), ())), precision=HIGH, preferred_element_type=F32
    )
    out_ref[rank:] = jnp.zeros((out_ref.shape[0] - rank, rank), F32)
    for copy in copies:
        copy.wait()
    for k in range(p_ref.shape[0]):
        both = (p_ref[k] + q_ref[k]) * f_ref[...]
        out_ref[rank + k : rank + k + 1] = jnp.sum(both, axis=0, keepdims=True)


def solve(x, columns, gram_c, first, second):
    count, rows, rank = first.shape
    square = jax.ShapeDtypeStruct((rank, rank), F32)
    return pl.pallas_call(
        solve_kernel,
        out_shape=[
            square,
            jax.ShapeDtypeStruct((rows, rank), F32),
            jax.ShapeDtypeStruct((rank + 8 * pl.cdiv(count, 8), rank), F32),
        ],
        in_specs=[SMEM] + [VMEM] * 5 + [HBM] * 2,
        out_specs=[VMEM] * 3,
        scratch_shapes=[
            pltpu.VMEM((count, rows, rank), F32),
            pltpu.VMEM((count, rows, rank), F32),
            pltpu.SemaphoreType.DMA((2,)),
        ],
        compiler_params=pltpu.CompilerParams(vmem_limit_bytes=12 << 20),
        name="solve",
    )(x, *columns, gram_c, first, second)


def swap(x, axis, bit=1):
    n = lax.axis_size(axis)
    return lax.ppermute(x, axis, [(i, i ^ bit) for i in range(n)])


def body(tensor, factor_a, factor_c, gram_c):
    mode_two, mode_three, mode_one = tensor.shape
    rank = factor_a.shape[1]
    core = lax.axis_index("c").astype(jnp.int32)
    x = lax.axis_index(RING).astype(jnp.int32)
    depth = lax.axis_size("z")
    half = mode_two // 2
    lanes = mode_one // 2
    flat = tensor.reshape(mode_two, mode_three, 2, lanes).transpose(0, 2, 1, 3)
    flat = flat.reshape(mode_two * mode_three * 2, lanes)
    flat, a_hbm, c_hbm = (
        pltpu.with_memory_space_constraint(v, pltpu.HBM) for v in (flat, factor_a, factor_c)
    )

    p_other, b_other = contract(jnp.stack([1 - core, x]), flat, a_hbm, c_hbm, half)
    p_mine, b_mine = contract(jnp.stack([core, x]), flat, a_hbm, c_hbm, half)
    gram_part = dot(factor_a.T, factor_a)
    at = x.reshape(1)
    sent = parcels(at, b_mine, swap(b_other, "c"), gram_part, swap(gram_part, "c"), depth)
    got = [sent[0]] + [swap(sent[n], RING, n) for n in (1, 2, 3)]
    column = (got[0] + got[1]) + (got[2] + got[3])
    column = spread(lax.all_to_all(column, "z", 0, 0))
    column = lax.all_to_all(column, "z", 0, 0)
    columns = [column] + [swap(column, RING, n) for n in (1, 2, 3)]
    gram_a, f_mine, sums = solve(at, columns, gram_c, p_mine, swap(p_other, "c"))

    sums = sums + swap(sums, "c")
    sums, f_mine = lax.optimization_barrier((sums, f_mine))
    parts = [sums] + [swap(sums, "y", bit) for bit in (1, 2, 3)]
    shape = (4, half // 4, rank)
    f_other = swap(f_mine, "c").reshape(shape)
    factor_b = assemble(jnp.stack([core, x]), f_mine.reshape(shape), f_other)
    parts[0], factor_b = lax.optimization_barrier((parts[0], factor_b))
    plane = ("z", "xl")
    spread_c = collect(parts, lax.axis_size(plane), mode_three)
    mttkrp_c = jnp.sum(lax.all_to_all(spread_c, plane, 0, 0), axis=0)
    factor_c_new = dot(mttkrp_c, inverse_of_product(gram_a, parts))
    return (factor_b.reshape(mode_two, rank), factor_c_new)


def solution(mesh):
    axes = (mesh.shape["ia"] // 4, 2, 2, mesh.shape["ja"], mesh.shape["ka"])
    fine = Mesh(mesh.devices.reshape(axes), ("z", "xl", "c", "y", "xh"))
    split = ("z", "xl", "c")
    placed = (P("y", "xh", split), P(split, None), P("xh", None), P())
    return jax.shard_map(
        body, mesh=fine, in_specs=placed, out_specs=(P("y", None), P("xh", None)), check_vma=False
    )
```

```python
import functools

import functools

import jax
import jax.numpy as jnp
from jax import lax
from jax.experimental import pallas as pl
from jax.experimental.pallas import tpu as pltpu
from jax.sharding import Mesh, PartitionSpec as P

HIGH = lax.Precision.HIGHEST
F32 = jnp.float32
BF16 = jnp.bfloat16
RING = ("xl", "xh")
VMEM = pl.BlockSpec(memory_space=pltpu.VMEM)
HBM = pl.BlockSpec(memory_space=pltpu.HBM)
SMEM = pl.BlockSpec(memory_space=pltpu.SMEM)


def dot(a, b):
    return jnp.dot(a, b, precision=HIGH, preferred_element_type=F32)


def mxu(a, b):
    return jnp.dot(a, b, preferred_element_type=F32)


def spd_inverse(a, step):
    n = a.shape[0]
    lane = lax.broadcasted_iota(jnp.int32, (step, n), 1)
    row_of = lax.broadcasted_iota(jnp.int32, (step, n), 0)
    lane_all = lax.broadcasted_iota(jnp.int32, (n, n), 1)
    zero = jnp.zeros((step, n), F32)
    for p in range(0, n, step):
        panel = a[p : p + step]
        columns = [jnp.broadcast_to(panel[:, p + c : p + c + 1], (step, n)) for c in range(step)]
        for c in range(step):
            column = columns[c]
            inverse = 1.0 / jnp.broadcast_to(column[c : c + 1], (step, n))
            pivot = row_of == c

            def eliminate(x):
                row = jnp.broadcast_to(x[c : c + 1], (step, n)) * inverse
                return jnp.where(pivot, row, x - column * row)

            panel = eliminate(jnp.where(lane == p + c, jnp.where(pivot, 1.0, 0.0), panel))
            for q in range(c + 1, step):
                columns[q] = eliminate(columns[q])
        spread = [zero] * (p // step) + [panel] + [zero] * ((n - p) // step - 1)
        rest = jnp.where((lane_all >= p) & (lane_all < p + step), 0.0, a)
        rest = rest - dot(a, jnp.concatenate(spread, axis=0))
        pieces = [rest[:p], panel, rest[p + step :]]
        a = jnp.concatenate([x for x in pieces if x.shape[0]], axis=0)
    return a


def total(refs, rows):
    first, second, third, fourth = (ref[rows] for ref in refs)
    return (first + second) + (third + fourth)


def collect_kernel(*refs):
    out_ref = refs[-1]
    count, rank = out_ref.shape[1:]
    part = total(refs[:-1], pl.ds(rank, count))
    out_ref[...] = jnp.broadcast_to(part[None], out_ref.shape)


def collect(parts, copies, count):
    rank = parts[0].shape[1]
    return pl.pallas_call(
        collect_kernel,
        out_shape=jax.ShapeDtypeStruct((copies, count, rank), F32),
        in_specs=[VMEM] * 4,
        out_specs=VMEM,
        compiler_params=pltpu.CompilerParams(vmem_limit_bytes=2 << 20),
        name="collect",
    )(*parts)


def inverse_kernel(first_ref, *refs):
    out_ref = refs[-1]
    second = total(refs[:-1], pl.ds(0, first_ref.shape[0]))
    out_ref[...] = spd_inverse(first_ref[...] * second, 16)


def inverse_of_product(first, parts):
    return pl.pallas_call(
        inverse_kernel,
        out_shape=jax.ShapeDtypeStruct(first.shape, F32),
        in_specs=[VMEM] * 5,
        out_specs=VMEM,
        compiler_params=pltpu.CompilerParams(vmem_limit_bytes=4 << 20),
        cost_estimate=pl.CostEstimate(flops=3 * 10**9, transcendentals=128, bytes_accessed=2**19),
        name="inverse_of_product",
    )(first, *parts)


def assemble_kernel(at_ref, mine_ref, other_ref, out_ref):
    count = mine_ref.shape[0]
    for n in range(count):
        out_ref[at_ref[0] * count + (at_ref[1] ^ n)] = mine_ref[n]
        out_ref[(1 - at_ref[0]) * count + (at_ref[1] ^ n)] = other_ref[n]


def assemble(at, mine, other):
    return pl.pallas_call(
        assemble_kernel,
        out_shape=jax.ShapeDtypeStruct((2 * mine.shape[0],) + mine.shape[1:], F32),
        in_specs=[SMEM, VMEM, VMEM],
        out_specs=VMEM,
        compiler_params=pltpu.CompilerParams(vmem_limit_bytes=8 << 20),
        name="assemble",
    )(at, mine, other)


def split3(x):
    high = x.astype(BF16)
    rest = x - high.astype(F32)
    middle = rest.astype(BF16)
    return high, middle, (rest - middle.astype(F32)).astype(BF16)


def contract_kernel(chunk, at_ref, x_hbm, a_hbm, c_hbm, p_ref, b_ref, *scratch):
    x_ref, w_ref, a_ref, c_ref, sems = scratch
    count, rows, rank = p_ref.shape
    span = 2 * count
    factors = [
        pltpu.make_async_copy(a_hbm, a_ref, sems.at[rows // chunk]),
        pltpu.make_async_copy(c_hbm, c_ref, sems.at[rows // chunk + 1]),
    ]
    factors[0].start()
    factors[1].start()
    copies = []
    for n, at in enumerate(range(0, rows, chunk)):
        size = chunk * span
        block = at_ref[0] * (rows // chunk) + (at_ref[1] ^ n)
        copy = pltpu.make_async_copy(
            x_hbm.at[pl.ds(block * size, size)], x_ref.at[pl.ds(at * span, size)], sems.at[n]
        )
        copy.start()
        copies.append(copy)
    factors[0].wait()
    factors[1].wait()
    for n, part in enumerate(split3(a_ref[...])):
        w_ref[:, n * rank : (n + 1) * rank] = part
    for n, at in enumerate(range(0, rows, chunk)):
        copies[n].wait()
        for row in range(at, at + chunk, 128):
            total = None
            for k in range(count):
                x = jnp.concatenate(
                    [
                        x_ref[pl.ds(row * span + k, 128, stride=span), :],
                        x_ref[pl.ds(row * span + count + k, 128, stride=span), :],
                    ],
                    axis=1,
                )
                high, middle, low = split3(x)
                wide = w_ref[:, : 2 * rank]
                y = mxu(high, wide) + mxu(middle, wide)
                small = mxu(low, w_ref[:, :rank]) + mxu(high, w_ref[:, 2 * rank :])
                value = y[:, :rank] + y[:, rank:] + small
                p_ref[k, row : row + 128] = value
                term = value * c_ref[k : k + 1, :]
                total = term if total is None else total + term
            b_ref[row : row + 128] = total


def contract(at, x, factor_a, factor_c, rows):
    count, (depth, rank) = factor_c.shape[0], factor_a.shape
    chunk = rows // 4
    return pl.pallas_call(
        functools.partial(contract_kernel, chunk),
        out_shape=[
            jax.ShapeDtypeStruct((count, rows, rank), F32),
            jax.ShapeDtypeStruct((rows, rank), F32),
        ],
        in_specs=[SMEM, HBM, HBM, HBM],
        out_specs=[VMEM, VMEM],
        scratch_shapes=[
            pltpu.VMEM((rows * 2 * count, depth // 2), F32),
            pltpu.VMEM((depth, 3 * rank), BF16),
            pltpu.VMEM((depth, rank), F32),
            pltpu.VMEM((count, rank), F32),
            pltpu.SemaphoreType.DMA((rows // chunk + 2,)),
        ],
        compiler_params=pltpu.CompilerParams(vmem_limit_bytes=12 << 20),
        cost_estimate=pl.CostEstimate(
            flops=16 * count * rows * depth * rank,
            transcendentals=0,
            bytes_accessed=4 * count * rows * (depth + rank),
        ),
        name="contract",
    )(at, x, factor_a, factor_c)


def parcels_kernel(x_ref, b_ref, b_far_ref, g_ref, g_far_ref, *outs):
    block, slab = b_ref.shape[0] // 4, g_ref.shape[0] // 4
    for n, out in enumerate(outs):
        at = pl.ds(n * block, block)
        out[:block] = b_ref[at] + b_far_ref[at]
        at = pl.ds(pl.multiple_of((x_ref[0] ^ n) * slab, slab), slab)
        out[block:] = 0.5 * (g_ref[at] + g_far_ref[at])


def parcels(x, b, b_far, g, g_far):
    shape = jax.ShapeDtypeStruct(((b.shape[0] + g.shape[0]) // 4, b.shape[1]), F32)
    return pl.pallas_call(
        parcels_kernel,
        out_shape=[shape] * 4,
        in_specs=[SMEM] + [VMEM] * 4,
        out_specs=[VMEM] * 4,
        compiler_params=pltpu.CompilerParams(vmem_limit_bytes=6 << 20),
        name="parcels",
    )(x, b, b_far, g, g_far)


def column_kernel(slab, *refs):
    out_ref = refs[-1]
    depth = out_ref.shape[0]
    block = refs[0].shape[0] - slab
    some, few = block // depth, slab // depth
    for z in range(depth):
        out_ref[z, :some] = total(refs[:-1], pl.ds(z * some, some))
        out_ref[z, some:] = total(refs[:-1], pl.ds(block + z * few, few))


def column_sum(parts, depth, slab):
    rows, rank = parts[0].shape
    return pl.pallas_call(
        functools.partial(column_kernel, slab),
        out_shape=jax.ShapeDtypeStruct((depth, rows // depth, rank), F32),
        in_specs=[VMEM] * 4,
        out_specs=VMEM,
        compiler_params=pltpu.CompilerParams(vmem_limit_bytes=2 << 20),
        name="column_sum",
    )(*parts)


def spread_kernel(x_ref, out_ref):
    out_ref[...] = jnp.broadcast_to(jnp.sum(x_ref[...], axis=0)[None], out_ref.shape)


def spread(x):
    return pl.pallas_call(
        spread_kernel,
        out_shape=jax.ShapeDtypeStruct(x.shape, F32),
        in_specs=[VMEM],
        out_specs=VMEM,
        compiler_params=pltpu.CompilerParams(vmem_limit_bytes=2 << 20),
        name="spread",
    )(x)


def flatten_kernel(x_ref, out_ref, *, slab):
    depth = x_ref.shape[0]
    block = out_ref.shape[0] - slab
    some, few = block // depth, slab // depth
    for z in range(depth):
        out_ref[z * some : (z + 1) * some] = x_ref[z, :some]
        at = block + z * few
        out_ref[at : at + few] = x_ref[z, some:]


def flatten(x, slab):
    depth, rows, rank = x.shape
    return pl.pallas_call(
        functools.partial(flatten_kernel, slab=slab),
        out_shape=jax.ShapeDtypeStruct((depth * rows, rank), F32),
        in_specs=[VMEM],
        out_specs=VMEM,
        compiler_params=pltpu.CompilerParams(vmem_limit_bytes=2 << 20),
        name="flatten",
    )(x)


def solve_kernel(x_ref, *refs):
    columns, (h_ref, p_ref, q_ref, g_ref, f_ref, out_ref) = refs[:4], refs[4:]
    rank = g_ref.shape[0]
    slab = rank // 4
    block = columns[0].shape[0] - slab
    for n in range(4):
        at = pl.multiple_of((x_ref[0] ^ n) * slab, slab)
        g_ref[pl.ds(at, slab)] = columns[n][block:]
    inverse = spd_inverse(g_ref[...] * h_ref[...], 16)
    for n in range(4):
        f = dot(columns[n][:block], inverse)
        f_ref[n * block : (n + 1) * block] = f
    f = f_ref[...]
    out_ref[:rank] = lax.dot_general(
        f, f, (((0,), (0,)), ((), ())), precision=HIGH, preferred_element_type=F32
    )
    out_ref[rank:] = jnp.zeros((out_ref.shape[0] - rank, rank), F32)
    for k in range(p_ref.shape[0]):
        both = (p_ref[k] + q_ref[k]) * f_ref[...]
        out_ref[rank + k : rank + k + 1] = jnp.sum(both, axis=0, keepdims=True)


def solve(x, columns, gram_c, first, second):
    count, rows, rank = first.shape
    square = jax.ShapeDtypeStruct((rank, rank), F32)
    return pl.pallas_call(
        solve_kernel,
        out_shape=[
            square,
            jax.ShapeDtypeStruct((rows, rank), F32),
            jax.ShapeDtypeStruct((rank + 8 * pl.cdiv(count, 8), rank), F32),
        ],
        in_specs=[SMEM] + [VMEM] * 7,
        out_specs=[VMEM] * 3,
        compiler_params=pltpu.CompilerParams(vmem_limit_bytes=12 << 20),
        name="solve",
    )(x, *columns, gram_c, first, second)


def swap(x, axis, bit=1):
    n = lax.axis_size(axis)
    return lax.ppermute(x, axis, [(i, i ^ bit) for i in range(n)])


def body(tensor, factor_a, factor_c, gram_c):
    mode_two, mode_three, mode_one = tensor.shape
    rank = factor_a.shape[1]
    core = lax.axis_index("c").astype(jnp.int32)
    x = lax.axis_index(RING).astype(jnp.int32)
    depth = lax.axis_size("z")
    half = mode_two // 2
    lanes = mode_one // 2
    flat = tensor.reshape(mode_two, mode_three, 2, lanes).transpose(0, 2, 1, 3)
    flat = flat.reshape(mode_two * mode_three * 2, lanes)
    flat, a_hbm, c_hbm = (
        pltpu.with_memory_space_constraint(v, pltpu.HBM) for v in (flat, factor_a, factor_c)
    )

    p_other, b_other = contract(jnp.stack([1 - core, x]), flat, a_hbm, c_hbm, half)
    p_mine, b_mine = contract(jnp.stack([core, x]), flat, a_hbm, c_hbm, half)
    gram_part = dot(factor_a.T, factor_a)
    at = x.reshape(1)
    sent = parcels(at, b_mine, swap(b_other, "c"), gram_part, swap(gram_part, "c"))
    got = [sent[0]] + [swap(sent[n], RING, n) for n in (1, 2, 3)]
    column = spread(lax.all_to_all(column_sum(got, depth, rank // 4), "z", 0, 0))
    column = flatten(lax.all_to_all(column, "z", 0, 0), rank // 4)
    columns = [column] + [swap(column, RING, n) for n in (1, 2, 3)]
    gram_a, f_mine, sums = solve(at, columns, gram_c, p_mine, swap(p_other, "c"))

    sums = sums + swap(sums, "c")
    sums, f_mine = lax.optimization_barrier((sums, f_mine))
    parts = [sums] + [swap(sums, "y", bit) for bit in (1, 2, 3)]
    shape = (4, half // 4, rank)
    f_other = swap(f_mine, "c").reshape(shape)
    factor_b = assemble(jnp.stack([core, x]), f_mine.reshape(shape), f_other)
    parts[0], factor_b = lax.optimization_barrier((parts[0], factor_b))
    plane = ("z", "xl")
    spread_c = collect(parts, lax.axis_size(plane), mode_three)
    mttkrp_c = jnp.sum(lax.all_to_all(spread_c, plane, 0, 0), axis=0)
    factor_c_new = dot(mttkrp_c, inverse_of_product(gram_a, parts))
    return (factor_b.reshape(mode_two, rank), factor_c_new)


def solution(mesh):
    axes = (mesh.shape["ia"] // 4, 2, 2, mesh.shape["ja"], mesh.shape["ka"])
    fine = Mesh(mesh.devices.reshape(axes), ("z", "xl", "c", "y", "xh"))
    split = ("z", "xl", "c")
    placed = (P("y", "xh", split), P(split, None), P("xh", None), P())
    return jax.shard_map(
        body, mesh=fine, in_specs=placed, out_specs=(P("y", None), P("xh", None)), check_vma=False
    )
```

```python
import functools

import functools

import jax
import jax.numpy as jnp
from jax import lax
from jax.experimental import pallas as pl
from jax.experimental.pallas import tpu as pltpu
from jax.sharding import Mesh, PartitionSpec as P

HIGH = lax.Precision.HIGHEST
F32 = jnp.float32
BF16 = jnp.bfloat16
RING = ("xl", "xh")
VMEM = pl.BlockSpec(memory_space=pltpu.VMEM)
HBM = pl.BlockSpec(memory_space=pltpu.HBM)
SMEM = pl.BlockSpec(memory_space=pltpu.SMEM)


def dot(a, b):
    return jnp.dot(a, b, precision=HIGH, preferred_element_type=F32)


def mxu(a, b):
    return jnp.dot(a, b, preferred_element_type=F32)


def spd_inverse(a, step):
    n = a.shape[0]
    lane = lax.broadcasted_iota(jnp.int32, (step, n), 1)
    row_of = lax.broadcasted_iota(jnp.int32, (step, n), 0)
    lane_all = lax.broadcasted_iota(jnp.int32, (n, n), 1)
    zero = jnp.zeros((step, n), F32)
    for p in range(0, n, step):
        panel = a[p : p + step]
        columns = [jnp.broadcast_to(panel[:, p + c : p + c + 1], (step, n)) for c in range(step)]
        for c in range(step):
            column = columns[c]
            inverse = 1.0 / jnp.broadcast_to(column[c : c + 1], (step, n))
            pivot = row_of == c

            def eliminate(x):
                row = jnp.broadcast_to(x[c : c + 1], (step, n)) * inverse
                return jnp.where(pivot, row, x - column * row)

            panel = eliminate(jnp.where(lane == p + c, jnp.where(pivot, 1.0, 0.0), panel))
            for q in range(c + 1, step):
                columns[q] = eliminate(columns[q])
        spread = [zero] * (p // step) + [panel] + [zero] * ((n - p) // step - 1)
        rest = jnp.where((lane_all >= p) & (lane_all < p + step), 0.0, a)
        rest = rest - dot(a, jnp.concatenate(spread, axis=0))
        pieces = [rest[:p], panel, rest[p + step :]]
        a = jnp.concatenate([x for x in pieces if x.shape[0]], axis=0)
    return a


def total(refs, rows):
    if len(refs) == 1:
        return refs[0][rows]
    first, second, third, fourth = (ref[rows] for ref in refs)
    return (first + second) + (third + fourth)


def collect_kernel(*refs):
    out_ref = refs[-1]
    count, rank = out_ref.shape[1:]
    part = total(refs[:-1], pl.ds(rank, count))
    out_ref[...] = jnp.broadcast_to(part[None], out_ref.shape)


def collect(parts, copies, count):
    rank = parts[0].shape[1]
    return pl.pallas_call(
        collect_kernel,
        out_shape=jax.ShapeDtypeStruct((copies, count, rank), F32),
        in_specs=[VMEM] * 4,
        out_specs=VMEM,
        compiler_params=pltpu.CompilerParams(vmem_limit_bytes=2 << 20),
        name="collect",
    )(*parts)


def inverse_kernel(first_ref, *refs):
    out_ref = refs[-1]
    second = total(refs[:-1], pl.ds(0, first_ref.shape[0]))
    out_ref[...] = spd_inverse(first_ref[...] * second, 16)


def inverse_of_product(first, parts):
    return pl.pallas_call(
        inverse_kernel,
        out_shape=jax.ShapeDtypeStruct(first.shape, F32),
        in_specs=[VMEM] * (1 + len(parts)),
        out_specs=VMEM,
        compiler_params=pltpu.CompilerParams(vmem_limit_bytes=4 << 20),
        cost_estimate=pl.CostEstimate(flops=3 * 10**9, transcendentals=128, bytes_accessed=2**19),
        name="inverse_of_product",
    )(first, *parts)


def assemble_kernel(at_ref, mine_ref, other_ref, out_ref):
    count = mine_ref.shape[0]
    for n in range(count):
        out_ref[at_ref[0] * count + (at_ref[1] ^ n)] = mine_ref[n]
        out_ref[(1 - at_ref[0]) * count + (at_ref[1] ^ n)] = other_ref[n]


def assemble(at, mine, other):
    return pl.pallas_call(
        assemble_kernel,
        out_shape=jax.ShapeDtypeStruct((2 * mine.shape[0],) + mine.shape[1:], F32),
        in_specs=[SMEM, VMEM, VMEM],
        out_specs=VMEM,
        compiler_params=pltpu.CompilerParams(vmem_limit_bytes=8 << 20),
        name="assemble",
    )(at, mine, other)


def split3(x):
    high = x.astype(BF16)
    rest = x - high.astype(F32)
    middle = rest.astype(BF16)
    return high, middle, (rest - middle.astype(F32)).astype(BF16)


def contract_kernel(chunk, at_ref, x_hbm, a_hbm, c_hbm, p_ref, b_ref, *scratch):
    x_ref, w_ref, a_ref, c_ref, sems = scratch
    count, rows, rank = p_ref.shape
    span = 2 * count
    factors = [
        pltpu.make_async_copy(a_hbm, a_ref, sems.at[rows // chunk]),
        pltpu.make_async_copy(c_hbm, c_ref, sems.at[rows // chunk + 1]),
    ]
    factors[0].start()
    factors[1].start()
    copies = []
    for n, at in enumerate(range(0, rows, chunk)):
        size = chunk * span
        block = at_ref[0] * (rows // chunk) + (at_ref[1] ^ n)
        copy = pltpu.make_async_copy(
            x_hbm.at[pl.ds(block * size, size)], x_ref.at[pl.ds(at * span, size)], sems.at[n]
        )
        copy.start()
        copies.append(copy)
    factors[0].wait()
    factors[1].wait()
    for n, part in enumerate(split3(a_ref[...])):
        w_ref[:, n * rank : (n + 1) * rank] = part
    for n, at in enumerate(range(0, rows, chunk)):
        copies[n].wait()
        for row in range(at, at + chunk, 128):
            total = None
            for k in range(count):
                x = jnp.concatenate(
                    [
                        x_ref[pl.ds(row * span + k, 128, stride=span), :],
                        x_ref[pl.ds(row * span + count + k, 128, stride=span), :],
                    ],
                    axis=1,
                )
                high, middle, low = split3(x)
                wide = w_ref[:, : 2 * rank]
                y = mxu(high, wide) + mxu(middle, wide)
                small = mxu(low, w_ref[:, :rank]) + mxu(high, w_ref[:, 2 * rank :])
                value = y[:, :rank] + y[:, rank:] + small
                p_ref[k, row : row + 128] = value
                term = value * c_ref[k : k + 1, :]
                total = term if total is None else total + term
            b_ref[row : row + 128] = total


def contract(at, x, factor_a, factor_c, rows):
    count, (depth, rank) = factor_c.shape[0], factor_a.shape
    chunk = rows // 4
    return pl.pallas_call(
        functools.partial(contract_kernel, chunk),
        out_shape=[
            jax.ShapeDtypeStruct((count, rows, rank), F32),
            jax.ShapeDtypeStruct((rows, rank), F32),
        ],
        in_specs=[SMEM, HBM, HBM, HBM],
        out_specs=[VMEM, VMEM],
        scratch_shapes=[
            pltpu.VMEM((rows * 2 * count, depth // 2), F32),
            pltpu.VMEM((depth, 3 * rank), BF16),
            pltpu.VMEM((depth, rank), F32),
            pltpu.VMEM((count, rank), F32),
            pltpu.SemaphoreType.DMA((rows // chunk + 2,)),
        ],
        compiler_params=pltpu.CompilerParams(vmem_limit_bytes=12 << 20),
        cost_estimate=pl.CostEstimate(
            flops=16 * count * rows * depth * rank,
            transcendentals=0,
            bytes_accessed=4 * count * rows * (depth + rank),
        ),
        name="contract",
    )(at, x, factor_a, factor_c)


def parcels_kernel(near_ref, far_ref, *outs):
    block = near_ref.shape[0] // 4
    for n, out in enumerate(outs):
        at = pl.ds(n * block, block)
        out[...] = near_ref[at] + far_ref[at]


def parcels(near, far):
    shape = jax.ShapeDtypeStruct((near.shape[0] // 4, near.shape[1]), F32)
    return pl.pallas_call(
        parcels_kernel,
        out_shape=[shape] * 4,
        in_specs=[VMEM] * 2,
        out_specs=[VMEM] * 4,
        compiler_params=pltpu.CompilerParams(vmem_limit_bytes=6 << 20),
        name="parcels",
    )(near, far)


def column_kernel(g_ref, g_far_ref, *refs):
    out_ref = refs[-1]
    depth = out_ref.shape[0]
    some, few = refs[0].shape[0] // depth, g_ref.shape[0] // depth
    for z in range(depth):
        out_ref[z, :some] = total(refs[:-1], pl.ds(z * some, some))
        at = pl.ds(z * few, few)
        out_ref[z, some:] = g_ref[at] + g_far_ref[at]


def column_sum(gram, gram_far, parts, depth):
    rank = gram.shape[1]
    rows = parts[0].shape[0] + gram.shape[0]
    return pl.pallas_call(
        column_kernel,
        out_shape=jax.ShapeDtypeStruct((depth, rows // depth, rank), F32),
        in_specs=[VMEM] * 6,
        out_specs=VMEM,
        compiler_params=pltpu.CompilerParams(vmem_limit_bytes=2 << 20),
        name="column_sum",
    )(gram, gram_far, *parts)


def spread_kernel(x_ref, out_ref):
    out_ref[...] = jnp.broadcast_to(jnp.sum(x_ref[...], axis=0)[None], out_ref.shape)


def spread(x):
    return pl.pallas_call(
        spread_kernel,
        out_shape=jax.ShapeDtypeStruct(x.shape, F32),
        in_specs=[VMEM],
        out_specs=VMEM,
        compiler_params=pltpu.CompilerParams(vmem_limit_bytes=2 << 20),
        name="spread",
    )(x)


def flatten_kernel(x_ref, m_ref, g_ref):
    depth = x_ref.shape[0]
    some, few = m_ref.shape[0] // depth, g_ref.shape[0] // depth
    for z in range(depth):
        m_ref[z * some : (z + 1) * some] = x_ref[z, :some]
        g_ref[z * few : (z + 1) * few] = x_ref[z, some:]


def flatten(x):
    depth, rows, rank = x.shape
    return pl.pallas_call(
        flatten_kernel,
        out_shape=[
            jax.ShapeDtypeStruct((depth * rows - rank, rank), F32),
            jax.ShapeDtypeStruct((rank, rank), F32),
        ],
        in_specs=[VMEM],
        out_specs=[VMEM] * 2,
        compiler_params=pltpu.CompilerParams(vmem_limit_bytes=2 << 20),
        name="flatten",
    )(x)


def solve_kernel(*refs):
    columns, (inv_ref, p_ref, q_ref, f_ref, out_ref) = refs[:4], refs[4:]
    rank = inv_ref.shape[0]
    block = columns[0].shape[0]
    for n in range(4):
        f = dot(columns[n][...], inv_ref[...])
        f_ref[n * block : (n + 1) * block] = f
    f = f_ref[...]
    out_ref[:rank] = lax.dot_general(
        f, f, (((0,), (0,)), ((), ())), precision=HIGH, preferred_element_type=F32
    )
    out_ref[rank:] = jnp.zeros((out_ref.shape[0] - rank, rank), F32)
    for k in range(p_ref.shape[0]):
        both = (p_ref[k] + q_ref[k]) * f_ref[...]
        out_ref[rank + k : rank + k + 1] = jnp.sum(both, axis=0, keepdims=True)


def solve(columns, inverse, first, second):
    count, rows, rank = first.shape
    return pl.pallas_call(
        solve_kernel,
        out_shape=[
            jax.ShapeDtypeStruct((rows, rank), F32),
            jax.ShapeDtypeStruct((rank + 8 * pl.cdiv(count, 8), rank), F32),
        ],
        in_specs=[VMEM] * 7,
        out_specs=[VMEM] * 2,
        compiler_params=pltpu.CompilerParams(vmem_limit_bytes=12 << 20),
        name="solve",
    )(*columns, inverse, first, second)


def swap(x, axis, bit=1):
    n = lax.axis_size(axis)
    return lax.ppermute(x, axis, [(i, i ^ bit) for i in range(n)])


def body(tensor, factor_a, factor_c, gram_c):
    mode_two, mode_three, mode_one = tensor.shape
    rank = factor_a.shape[1]
    core = lax.axis_index("c").astype(jnp.int32)
    x = lax.axis_index(RING).astype(jnp.int32)
    depth = lax.axis_size("z")
    half = mode_two // 2
    lanes = mode_one // 2
    flat = tensor.reshape(mode_two, mode_three, 2, lanes).transpose(0, 2, 1, 3)
    flat = flat.reshape(mode_two * mode_three * 2, lanes)
    flat, a_hbm, c_hbm = (
        pltpu.with_memory_space_constraint(v, pltpu.HBM) for v in (flat, factor_a, factor_c)
    )

    p_other, b_other = contract(jnp.stack([1 - core, x]), flat, a_hbm, c_hbm, half)
    p_mine, b_mine = contract(jnp.stack([core, x]), flat, a_hbm, c_hbm, half)
    gram_part = dot(factor_a.T, factor_a)
    gram_part = gram_part + swap(gram_part, "c")
    sent = parcels(b_mine, swap(b_other, "c"))
    got = [sent[0]] + [swap(sent[n], RING, n) for n in (1, 2, 3)]
    column = column_sum(gram_part, swap(gram_part, "xl"), got, depth)
    column = spread(lax.all_to_all(column, "z", 0, 0))
    column, gram_a = flatten(lax.all_to_all(column, "z", 0, 0))
    columns = [column] + [swap(column, RING, n) for n in (1, 2, 3)]
    inverse = inverse_of_product(gram_a, [gram_c])
    f_mine, sums = solve(columns, inverse, p_mine, swap(p_other, "c"))

    sums = sums + swap(sums, "c")
    sums, f_mine = lax.optimization_barrier((sums, f_mine))
    parts = [sums] + [swap(sums, "y", bit) for bit in (1, 2, 3)]
    shape = (4, half // 4, rank)
    f_other = swap(f_mine, "c").reshape(shape)
    factor_b = assemble(jnp.stack([core, x]), f_mine.reshape(shape), f_other)
    parts[0], factor_b = lax.optimization_barrier((parts[0], factor_b))
    plane = ("z", "xl")
    spread_c = collect(parts, lax.axis_size(plane), mode_three)
    mttkrp_c = jnp.sum(lax.all_to_all(spread_c, plane, 0, 0), axis=0)
    factor_c_new = dot(mttkrp_c, inverse_of_product(gram_a, parts))
    return (factor_b.reshape(mode_two, rank), factor_c_new)


def solution(mesh):
    axes = (mesh.shape["ia"] // 4, 2, 2, mesh.shape["ja"], mesh.shape["ka"])
    fine = Mesh(mesh.devices.reshape(axes), ("z", "xl", "c", "y", "xh"))
    split = ("z", "xl", "c")
    placed = (P("y", "xh", split), P(split, None), P("xh", None), P())
    return jax.shard_map(
        body, mesh=fine, in_specs=placed, out_specs=(P("y", None), P("xh", None)), check_vma=False
    )
```

```python
import functools

import functools

import jax
import jax.numpy as jnp
from jax import lax
from jax.experimental import pallas as pl
from jax.experimental.pallas import tpu as pltpu
from jax.sharding import Mesh, PartitionSpec as P

HIGH = lax.Precision.HIGHEST
F32 = jnp.float32
BF16 = jnp.bfloat16
RING = ("xl", "xh")
VMEM = pl.BlockSpec(memory_space=pltpu.VMEM)
HBM = pl.BlockSpec(memory_space=pltpu.HBM)
SMEM = pl.BlockSpec(memory_space=pltpu.SMEM)


def dot(a, b):
    return jnp.dot(a, b, precision=HIGH, preferred_element_type=F32)


def mxu(a, b):
    return jnp.dot(a, b, preferred_element_type=F32)


def spd_inverse(a, step):
    n = a.shape[0]
    lane = lax.broadcasted_iota(jnp.int32, (step, n), 1)
    row_of = lax.broadcasted_iota(jnp.int32, (step, n), 0)
    lane_all = lax.broadcasted_iota(jnp.int32, (n, n), 1)
    zero = jnp.zeros((step, n), F32)
    for p in range(0, n, step):
        panel = a[p : p + step]
        columns = [jnp.broadcast_to(panel[:, p + c : p + c + 1], (step, n)) for c in range(step)]
        for c in range(step):
            column = columns[c]
            inverse = 1.0 / jnp.broadcast_to(column[c : c + 1], (step, n))
            pivot = row_of == c

            def eliminate(x):
                row = jnp.broadcast_to(x[c : c + 1], (step, n)) * inverse
                return jnp.where(pivot, row, x - column * row)

            panel = eliminate(jnp.where(lane == p + c, jnp.where(pivot, 1.0, 0.0), panel))
            for q in range(c + 1, step):
                columns[q] = eliminate(columns[q])
        spread = [zero] * (p // step) + [panel] + [zero] * ((n - p) // step - 1)
        rest = jnp.where((lane_all >= p) & (lane_all < p + step), 0.0, a)
        rest = rest - dot(a, jnp.concatenate(spread, axis=0))
        pieces = [rest[:p], panel, rest[p + step :]]
        a = jnp.concatenate([x for x in pieces if x.shape[0]], axis=0)
    return a


def total(refs, rows):
    if len(refs) == 1:
        return refs[0][rows]
    if len(refs) == 2:
        return refs[0][rows] + refs[1][rows]
    first, second, third, fourth = (ref[rows] for ref in refs)
    return (first + second) + (third + fourth)


def collect_kernel(*refs):
    parts, (out_ref, g_ref) = refs[:4], refs[4:]
    count, rank = out_ref.shape[1:]
    part = total(parts, pl.ds(rank, count))
    out_ref[...] = jnp.broadcast_to(part[None], out_ref.shape)
    g_ref[...] = total(parts, pl.ds(0, rank))


def collect(parts, copies, count):
    rank = parts[0].shape[1]
    return pl.pallas_call(
        collect_kernel,
        out_shape=[
            jax.ShapeDtypeStruct((copies, count, rank), F32),
            jax.ShapeDtypeStruct((rank, rank), F32),
        ],
        in_specs=[VMEM] * 4,
        out_specs=[VMEM] * 2,
        compiler_params=pltpu.CompilerParams(vmem_limit_bytes=2 << 20),
        name="collect",
    )(*parts)


def inverse_kernel(first_ref, *refs):
    out_ref = refs[-1]
    second = total(refs[:-1], pl.ds(0, first_ref.shape[0]))
    out_ref[...] = spd_inverse(first_ref[...] * second, 16)


def inverse_of_product(first, parts):
    return pl.pallas_call(
        inverse_kernel,
        out_shape=jax.ShapeDtypeStruct(first.shape, F32),
        in_specs=[VMEM] * (1 + len(parts)),
        out_specs=VMEM,
        compiler_params=pltpu.CompilerParams(vmem_limit_bytes=4 << 20),
        cost_estimate=pl.CostEstimate(flops=3 * 10**9, transcendentals=128, bytes_accessed=2**19),
        name="inverse_of_product",
    )(first, *parts)


def assemble_kernel(at_ref, mine_ref, other_ref, out_ref):
    count = mine_ref.shape[0]
    for n in range(count):
        out_ref[at_ref[0] * count + (at_ref[1] ^ n)] = mine_ref[n]
        out_ref[(1 - at_ref[0]) * count + (at_ref[1] ^ n)] = other_ref[n]


def assemble(at, mine, other):
    return pl.pallas_call(
        assemble_kernel,
        out_shape=jax.ShapeDtypeStruct((2 * mine.shape[0],) + mine.shape[1:], F32),
        in_specs=[SMEM, VMEM, VMEM],
        out_specs=VMEM,
        compiler_params=pltpu.CompilerParams(vmem_limit_bytes=8 << 20),
        name="assemble",
    )(at, mine, other)


def split3(x):
    high = x.astype(BF16)
    rest = x - high.astype(F32)
    middle = rest.astype(BF16)
    return high, middle, (rest - middle.astype(F32)).astype(BF16)


def contract_kernel(chunk, at_ref, x_hbm, a_hbm, c_hbm, p_ref, b_ref, *scratch):
    x_ref, w_ref, a_ref, c_ref, sems = scratch
    count, rows, rank = p_ref.shape
    span = 2 * count
    factors = [
        pltpu.make_async_copy(a_hbm, a_ref, sems.at[rows // chunk]),
        pltpu.make_async_copy(c_hbm, c_ref, sems.at[rows // chunk + 1]),
    ]
    factors[0].start()
    factors[1].start()
    copies = []
    for n, at in enumerate(range(0, rows, chunk)):
        size = chunk * span
        block = at_ref[0] * (rows // chunk) + (at_ref[1] ^ n)
        copy = pltpu.make_async_copy(
            x_hbm.at[pl.ds(block * size, size)], x_ref.at[pl.ds(at * span, size)], sems.at[n]
        )
        copy.start()
        copies.append(copy)
    factors[0].wait()
    factors[1].wait()
    for n, part in enumerate(split3(a_ref[...])):
        w_ref[:, n * rank : (n + 1) * rank] = part
    for n, at in enumerate(range(0, rows, chunk)):
        copies[n].wait()
        for row in range(at, at + chunk, 128):
            total = None
            for k in range(count):
                x = jnp.concatenate(
                    [
                        x_ref[pl.ds(row * span + k, 128, stride=span), :],
                        x_ref[pl.ds(row * span + count + k, 128, stride=span), :],
                    ],
                    axis=1,
                )
                high, middle, low = split3(x)
                wide = w_ref[:, : 2 * rank]
                y = mxu(high, wide) + mxu(middle, wide)
                small = mxu(low, w_ref[:, :rank]) + mxu(high, w_ref[:, 2 * rank :])
                value = y[:, :rank] + y[:, rank:] + small
                p_ref[k, row : row + 128] = value
                term = value * c_ref[k : k + 1, :]
                total = term if total is None else total + term
            b_ref[row : row + 128] = total


def contract(at, x, factor_a, factor_c, rows):
    count, (depth, rank) = factor_c.shape[0], factor_a.shape
    chunk = rows // 4
    return pl.pallas_call(
        functools.partial(contract_kernel, chunk),
        out_shape=[
            jax.ShapeDtypeStruct((count, rows, rank), F32),
            jax.ShapeDtypeStruct((rows, rank), F32),
        ],
        in_specs=[SMEM, HBM, HBM, HBM],
        out_specs=[VMEM, VMEM],
        scratch_shapes=[
            pltpu.VMEM((rows * 2 * count, depth // 2), F32),
            pltpu.VMEM((depth, 3 * rank), BF16),
            pltpu.VMEM((depth, rank), F32),
            pltpu.VMEM((count, rank), F32),
            pltpu.SemaphoreType.DMA((rows // chunk + 2,)),
        ],
        compiler_params=pltpu.CompilerParams(vmem_limit_bytes=12 << 20),
        cost_estimate=pl.CostEstimate(
            flops=16 * count * rows * depth * rank,
            transcendentals=0,
            bytes_accessed=4 * count * rows * (depth + rank),
        ),
        name="contract",
    )(at, x, factor_a, factor_c)


def parcels_kernel(near_ref, far_ref, *outs):
    block = near_ref.shape[0] // 4
    for n, out in enumerate(outs):
        at = pl.ds(n * block, block)
        out[...] = near_ref[at] + far_ref[at]


def parcels(near, far):
    shape = jax.ShapeDtypeStruct((near.shape[0] // 4, near.shape[1]), F32)
    return pl.pallas_call(
        parcels_kernel,
        out_shape=[shape] * 4,
        in_specs=[VMEM] * 2,
        out_specs=[VMEM] * 4,
        compiler_params=pltpu.CompilerParams(vmem_limit_bytes=6 << 20),
        name="parcels",
    )(near, far)


def column_kernel(g_ref, g_far_ref, *refs):
    out_ref = refs[-1]
    depth = out_ref.shape[0]
    some, few = refs[0].shape[0] // depth, g_ref.shape[0] // depth
    for z in range(depth):
        out_ref[z, :some] = total(refs[:-1], pl.ds(z * some, some))
        at = pl.ds(z * few, few)
        out_ref[z, some:] = g_ref[at] + g_far_ref[at]


def column_sum(gram, gram_far, parts, depth):
    rank = gram.shape[1]
    rows = parts[0].shape[0] + gram.shape[0]
    return pl.pallas_call(
        column_kernel,
        out_shape=jax.ShapeDtypeStruct((depth, rows // depth, rank), F32),
        in_specs=[VMEM] * 6,
        out_specs=VMEM,
        compiler_params=pltpu.CompilerParams(vmem_limit_bytes=2 << 20),
        name="column_sum",
    )(gram, gram_far, *parts)


def spread_kernel(x_ref, out_ref):
    out_ref[...] = jnp.broadcast_to(jnp.sum(x_ref[...], axis=0)[None], out_ref.shape)


def spread(x):
    return pl.pallas_call(
        spread_kernel,
        out_shape=jax.ShapeDtypeStruct(x.shape, F32),
        in_specs=[VMEM],
        out_specs=VMEM,
        compiler_params=pltpu.CompilerParams(vmem_limit_bytes=2 << 20),
        name="spread",
    )(x)


def flatten_kernel(x_ref, m_ref, g_ref):
    depth = x_ref.shape[0]
    some, few = m_ref.shape[0] // depth, g_ref.shape[0] // depth
    for z in range(depth):
        m_ref[z * some : (z + 1) * some] = x_ref[z, :some]
        g_ref[z * few : (z + 1) * few] = x_ref[z, some:]


def flatten(x):
    depth, rows, rank = x.shape
    return pl.pallas_call(
        flatten_kernel,
        out_shape=[
            jax.ShapeDtypeStruct((depth * rows - rank, rank), F32),
            jax.ShapeDtypeStruct((rank, rank), F32),
        ],
        in_specs=[VMEM],
        out_specs=[VMEM] * 2,
        compiler_params=pltpu.CompilerParams(vmem_limit_bytes=2 << 20),
        name="flatten",
    )(x)


def solve_kernel(*refs):
    columns, (inv_ref, p_ref, q_ref, f_ref, out_ref) = refs[:4], refs[4:]
    rank = inv_ref.shape[0]
    block = columns[0].shape[0]
    for n in range(4):
        f = dot(columns[n][...], inv_ref[...])
        f_ref[n * block : (n + 1) * block] = f
    f = f_ref[...]
    out_ref[:rank] = lax.dot_general(
        f, f, (((0,), (0,)), ((), ())), precision=HIGH, preferred_element_type=F32
    )
    out_ref[rank:] = jnp.zeros((out_ref.shape[0] - rank, rank), F32)
    for k in range(p_ref.shape[0]):
        both = (p_ref[k] + q_ref[k]) * f_ref[...]
        out_ref[rank + k : rank + k + 1] = jnp.sum(both, axis=0, keepdims=True)


def solve(columns, inverse, first, second):
    count, rows, rank = first.shape
    return pl.pallas_call(
        solve_kernel,
        out_shape=[
            jax.ShapeDtypeStruct((rows, rank), F32),
            jax.ShapeDtypeStruct((rank + 8 * pl.cdiv(count, 8), rank), F32),
        ],
        in_specs=[VMEM] * 7,
        out_specs=[VMEM] * 2,
        compiler_params=pltpu.CompilerParams(vmem_limit_bytes=12 << 20),
        name="solve",
    )(*columns, inverse, first, second)


def swap(x, axis, bit=1):
    n = lax.axis_size(axis)
    return lax.ppermute(x, axis, [(i, i ^ bit) for i in range(n)])


def body(tensor, factor_a, factor_c, gram_c):
    mode_two, mode_three, mode_one = tensor.shape
    rank = factor_a.shape[1]
    core = lax.axis_index("c").astype(jnp.int32)
    x = lax.axis_index(RING).astype(jnp.int32)
    depth = lax.axis_size("z")
    half = mode_two // 2
    lanes = mode_one // 2
    flat = tensor.reshape(mode_two, mode_three, 2, lanes).transpose(0, 2, 1, 3)
    flat = flat.reshape(mode_two * mode_three * 2, lanes)
    flat, a_hbm, c_hbm = (
        pltpu.with_memory_space_constraint(v, pltpu.HBM) for v in (flat, factor_a, factor_c)
    )

    p_other, b_other = contract(jnp.stack([1 - core, x]), flat, a_hbm, c_hbm, half)
    p_mine, b_mine = contract(jnp.stack([core, x]), flat, a_hbm, c_hbm, half)
    gram_part = dot(factor_a.T, factor_a)
    gram_part = gram_part + swap(gram_part, "c")
    sent = parcels(b_mine, swap(b_other, "c"))
    got = [sent[0]] + [swap(sent[n], RING, n) for n in (1, 2, 3)]
    column = column_sum(gram_part, swap(gram_part, "xl"), got, depth)
    column = spread(lax.all_to_all(column, "z", 0, 0))
    column, gram_a = flatten(lax.all_to_all(column, "z", 0, 0))
    columns = [column] + [swap(column, RING, n) for n in (1, 2, 3)]
    inverse = inverse_of_product(gram_a, [gram_c])
    f_mine, sums = solve(columns, inverse, p_mine, swap(p_other, "c"))

    parts = [sums] + [swap(sums, "y", bit) for bit in (1, 2, 3)]
    shape = (4, half // 4, rank)
    f_other = swap(f_mine, "c").reshape(shape)
    factor_b = assemble(jnp.stack([core, x]), f_mine.reshape(shape), f_other)
    parts[0], factor_b = lax.optimization_barrier((parts[0], factor_b))
    split = ("z", "xl", "c")
    spread_c, gram_b = collect(parts, lax.axis_size(split), mode_three)
    gram_far = swap(gram_b, "c")
    mttkrp_c = jnp.sum(lax.all_to_all(spread_c, split, 0, 0), axis=0)
    factor_c_new = dot(mttkrp_c, inverse_of_product(gram_a, [gram_b, gram_far]))
    return (factor_b.reshape(mode_two, rank), factor_c_new)


def solution(mesh):
    axes = (mesh.shape["ia"] // 4, 2, 2, mesh.shape["ja"], mesh.shape["ka"])
    fine = Mesh(mesh.devices.reshape(axes), ("z", "xl", "c", "y", "xh"))
    split = ("z", "xl", "c")
    placed = (P("y", "xh", split), P(split, None), P("xh", None), P())
    return jax.shard_map(
        body, mesh=fine, in_specs=placed, out_specs=(P("y", None), P("xh", None)), check_vma=False
    )
```

```python
import functools

import functools

import jax
import jax.numpy as jnp
from jax import lax
from jax.experimental import pallas as pl
from jax.experimental.pallas import tpu as pltpu
from jax.sharding import Mesh, PartitionSpec as P

HIGH = lax.Precision.HIGHEST
F32 = jnp.float32
BF16 = jnp.bfloat16
RING = ("xl", "xh")
VMEM = pl.BlockSpec(memory_space=pltpu.VMEM)
HBM = pl.BlockSpec(memory_space=pltpu.HBM)
SMEM = pl.BlockSpec(memory_space=pltpu.SMEM)


def dot(a, b):
    return jnp.dot(a, b, precision=HIGH, preferred_element_type=F32)


def mxu(a, b):
    return jnp.dot(a, b, preferred_element_type=F32)


def spd_inverse(a, step):
    n = a.shape[0]
    lane = lax.broadcasted_iota(jnp.int32, (step, n), 1)
    row_of = lax.broadcasted_iota(jnp.int32, (step, n), 0)
    lane_all = lax.broadcasted_iota(jnp.int32, (n, n), 1)
    zero = jnp.zeros((step, n), F32)
    for p in range(0, n, step):
        panel = a[p : p + step]
        columns = [jnp.broadcast_to(panel[:, p + c : p + c + 1], (step, n)) for c in range(step)]
        for c in range(step):
            column = columns[c]
            inverse = 1.0 / jnp.broadcast_to(column[c : c + 1], (step, n))
            pivot = row_of == c

            def eliminate(x):
                row = jnp.broadcast_to(x[c : c + 1], (step, n)) * inverse
                return jnp.where(pivot, row, x - column * row)

            panel = eliminate(jnp.where(lane == p + c, jnp.where(pivot, 1.0, 0.0), panel))
            for q in range(c + 1, step):
                columns[q] = eliminate(columns[q])
        spread = [zero] * (p // step) + [panel] + [zero] * ((n - p) // step - 1)
        rest = jnp.where((lane_all >= p) & (lane_all < p + step), 0.0, a)
        rest = rest - dot(a, jnp.concatenate(spread, axis=0))
        pieces = [rest[:p], panel, rest[p + step :]]
        a = jnp.concatenate([x for x in pieces if x.shape[0]], axis=0)
    return a


def total(refs, rows):
    if len(refs) == 1:
        return refs[0][rows]
    first, second, third, fourth = (ref[rows] for ref in refs)
    return (first + second) + (third + fourth)


def collect_kernel(*refs):
    out_ref = refs[-1]
    count, rank = out_ref.shape[1:]
    part = total(refs[:-1], pl.ds(rank, count))
    out_ref[...] = jnp.broadcast_to(part[None], out_ref.shape)


def collect(parts, copies, count):
    rank = parts[0].shape[1]
    return pl.pallas_call(
        collect_kernel,
        out_shape=jax.ShapeDtypeStruct((copies, count, rank), F32),
        in_specs=[VMEM] * 4,
        out_specs=VMEM,
        compiler_params=pltpu.CompilerParams(vmem_limit_bytes=2 << 20),
        name="collect",
    )(*parts)


def inverse_kernel(first_ref, *refs):
    out_ref = refs[-1]
    second = total(refs[:-1], pl.ds(0, first_ref.shape[0]))
    out_ref[...] = spd_inverse(first_ref[...] * second, 16)


def inverse_of_product(first, parts):
    return pl.pallas_call(
        inverse_kernel,
        out_shape=jax.ShapeDtypeStruct(first.shape, F32),
        in_specs=[VMEM] * (1 + len(parts)),
        out_specs=VMEM,
        compiler_params=pltpu.CompilerParams(vmem_limit_bytes=4 << 20),
        cost_estimate=pl.CostEstimate(flops=3 * 10**9, transcendentals=128, bytes_accessed=2**19),
        name="inverse_of_product",
    )(first, *parts)


def product_kernel(x_ref, inv_ref, out_ref):
    out_ref[...] = dot(jnp.sum(x_ref[...], axis=0), inv_ref[...])


def product(x, inverse):
    return pl.pallas_call(
        product_kernel,
        out_shape=jax.ShapeDtypeStruct(x.shape[1:], F32),
        in_specs=[VMEM] * 2,
        out_specs=VMEM,
        compiler_params=pltpu.CompilerParams(vmem_limit_bytes=2 << 20),
        name="product",
    )(x, inverse)


def assemble_kernel(at_ref, mine_ref, other_ref, out_ref):
    count = mine_ref.shape[0]
    for n in range(count):
        out_ref[at_ref[0] * count + (at_ref[1] ^ n)] = mine_ref[n]
        out_ref[(1 - at_ref[0]) * count + (at_ref[1] ^ n)] = other_ref[n]


def assemble(at, mine, other):
    return pl.pallas_call(
        assemble_kernel,
        out_shape=jax.ShapeDtypeStruct((2 * mine.shape[0],) + mine.shape[1:], F32),
        in_specs=[SMEM, VMEM, VMEM],
        out_specs=VMEM,
        compiler_params=pltpu.CompilerParams(vmem_limit_bytes=8 << 20),
        name="assemble",
    )(at, mine, other)


def split3(x):
    high = x.astype(BF16)
    rest = x - high.astype(F32)
    middle = rest.astype(BF16)
    return high, middle, (rest - middle.astype(F32)).astype(BF16)


def contract_kernel(chunk, resident, at_ref, x_hbm, a_in, c_in, p_ref, b_ref, *scratch):
    x_ref, w_ref, a_ref, c_ref, sems = scratch
    if resident:
        a_ref, c_ref = a_in, c_in
    count, rows, rank = p_ref.shape
    span = 2 * count
    factors = []
    if not resident:
        for n, (source, target) in enumerate(((a_in, a_ref), (c_in, c_ref))):
            factors.append(pltpu.make_async_copy(source, target, sems.at[rows // chunk + n]))
            factors[n].start()
    part_rows = min(256, chunk)
    copies = []
    for n, at in enumerate(range(0, rows, chunk)):
        size = chunk * span
        block = at_ref[0] * (rows // chunk) + (at_ref[1] ^ n)
        copy = pltpu.make_async_copy(
            x_hbm.at[pl.ds(block * size, size)], x_ref.at[pl.ds(at * span, size)], sems.at[n]
        )
        copy.start()
        copies.append(copy)
    for copy in factors:
        copy.wait()
    for n, part in enumerate(split3(a_ref[...])):
        w_ref[:, n * rank : (n + 1) * rank] = part
    for n, at in enumerate(range(0, rows, chunk)):
        copies[n].wait()
        for row in range(at, at + chunk, part_rows):
            total = None
            for k in range(count):
                x = jnp.concatenate(
                    [
                        x_ref[pl.ds(row * span + k, part_rows, stride=span), :],
                        x_ref[pl.ds(row * span + count + k, part_rows, stride=span), :],
                    ],
                    axis=1,
                )
                high, middle, low = split3(x)
                wide = w_ref[:, : 2 * rank]
                y = mxu(high, wide) + mxu(middle, wide)
                small = mxu(low, w_ref[:, :rank]) + mxu(high, w_ref[:, 2 * rank :])
                value = y[:, :rank] + y[:, rank:] + small
                p_ref[k, row : row + part_rows] = value
                term = value * c_ref[k : k + 1, :]
                total = term if total is None else total + term
            b_ref[row : row + part_rows] = total


def contract(at, x, factor_a, factor_c, rows, resident):
    count, (depth, rank) = factor_c.shape[0], factor_a.shape
    chunk = rows // 4
    return pl.pallas_call(
        functools.partial(contract_kernel, chunk, resident),
        out_shape=[
            jax.ShapeDtypeStruct((count, rows, rank), F32),
            jax.ShapeDtypeStruct((rows, rank), F32),
        ],
        in_specs=[SMEM, HBM] + [VMEM if resident else HBM] * 2,
        out_specs=[VMEM, VMEM],
        scratch_shapes=[
            pltpu.VMEM((rows * 2 * count, depth // 2), F32),
            pltpu.VMEM((depth, 3 * rank), BF16),
            pltpu.VMEM((depth, rank), F32),
            pltpu.VMEM((count, rank), F32),
            pltpu.SemaphoreType.DMA((rows // chunk + 2,)),
        ],
        compiler_params=pltpu.CompilerParams(vmem_limit_bytes=12 << 20),
        cost_estimate=pl.CostEstimate(
            flops=16 * count * rows * depth * rank,
            transcendentals=0,
            bytes_accessed=4 * count * rows * (depth + rank),
        ),
        name="contract",
    )(at, x, factor_a, factor_c)


def parcels_kernel(near_ref, far_ref, *outs):
    block = near_ref.shape[0] // 4
    for n, out in enumerate(outs):
        at = pl.ds(n * block, block)
        out[...] = near_ref[at] + far_ref[at]


def parcels(near, far):
    shape = jax.ShapeDtypeStruct((near.shape[0] // 4, near.shape[1]), F32)
    return pl.pallas_call(
        parcels_kernel,
        out_shape=[shape] * 4,
        in_specs=[VMEM] * 2,
        out_specs=[VMEM] * 4,
        compiler_params=pltpu.CompilerParams(vmem_limit_bytes=6 << 20),
        name="parcels",
    )(near, far)


def column_kernel(g_ref, g_far_ref, *refs):
    out_ref = refs[-1]
    depth = out_ref.shape[0]
    some, few = refs[0].shape[0] // depth, g_ref.shape[0] // depth
    for z in range(depth):
        out_ref[z, :some] = total(refs[:-1], pl.ds(z * some, some))
        at = pl.ds(z * few, few)
        out_ref[z, some:] = g_ref[at] + g_far_ref[at]


def column_sum(gram, gram_far, parts, depth):
    rank = gram.shape[1]
    rows = parts[0].shape[0] + gram.shape[0]
    return pl.pallas_call(
        column_kernel,
        out_shape=jax.ShapeDtypeStruct((depth, rows // depth, rank), F32),
        in_specs=[VMEM] * 6,
        out_specs=VMEM,
        compiler_params=pltpu.CompilerParams(vmem_limit_bytes=2 << 20),
        name="column_sum",
    )(gram, gram_far, *parts)


def spread_kernel(x_ref, out_ref):
    out_ref[...] = jnp.broadcast_to(jnp.sum(x_ref[...], axis=0)[None], out_ref.shape)


def spread(x):
    return pl.pallas_call(
        spread_kernel,
        out_shape=jax.ShapeDtypeStruct(x.shape, F32),
        in_specs=[VMEM],
        out_specs=VMEM,
        compiler_params=pltpu.CompilerParams(vmem_limit_bytes=2 << 20),
        name="spread",
    )(x)


def flatten_kernel(x_ref, m_ref, g_ref):
    depth = x_ref.shape[0]
    some, few = m_ref.shape[0] // depth, g_ref.shape[0] // depth
    for z in range(depth):
        m_ref[z * some : (z + 1) * some] = x_ref[z, :some]
        g_ref[z * few : (z + 1) * few] = x_ref[z, some:]


def flatten(x):
    depth, rows, rank = x.shape
    return pl.pallas_call(
        flatten_kernel,
        out_shape=[
            jax.ShapeDtypeStruct((depth * rows - rank, rank), F32),
            jax.ShapeDtypeStruct((rank, rank), F32),
        ],
        in_specs=[VMEM],
        out_specs=[VMEM] * 2,
        compiler_params=pltpu.CompilerParams(vmem_limit_bytes=2 << 20),
        name="flatten",
    )(x)


def solve_kernel(*refs):
    columns, (inv_ref, p_ref, q_ref, f_ref, out_ref) = refs[:4], refs[4:]
    rank = inv_ref.shape[0]
    block = columns[0].shape[0]
    for n in range(4):
        f = dot(columns[n][...], inv_ref[...])
        f_ref[n * block : (n + 1) * block] = f
    f = f_ref[...]
    out_ref[:rank] = lax.dot_general(
        f, f, (((0,), (0,)), ((), ())), precision=HIGH, preferred_element_type=F32
    )
    out_ref[rank:] = jnp.zeros((out_ref.shape[0] - rank, rank), F32)
    for k in range(p_ref.shape[0]):
        both = (p_ref[k] + q_ref[k]) * f_ref[...]
        out_ref[rank + k : rank + k + 1] = jnp.sum(both, axis=0, keepdims=True)


def solve(columns, inverse, first, second):
    count, rows, rank = first.shape
    return pl.pallas_call(
        solve_kernel,
        out_shape=[
            jax.ShapeDtypeStruct((rows, rank), F32),
            jax.ShapeDtypeStruct((rank + 8 * pl.cdiv(count, 8), rank), F32),
        ],
        in_specs=[VMEM] * 7,
        out_specs=[VMEM] * 2,
        compiler_params=pltpu.CompilerParams(vmem_limit_bytes=12 << 20),
        name="solve",
    )(*columns, inverse, first, second)


def swap(x, axis, bit=1):
    n = lax.axis_size(axis)
    return lax.ppermute(x, axis, [(i, i ^ bit) for i in range(n)])


def body(tensor, factor_a, factor_c, gram_c):
    mode_two, mode_three, mode_one = tensor.shape
    rank = factor_a.shape[1]
    core = lax.axis_index("c").astype(jnp.int32)
    x = lax.axis_index(RING).astype(jnp.int32)
    depth = lax.axis_size("z")
    half = mode_two // 2
    lanes = mode_one // 2
    flat = tensor.reshape(mode_two, mode_three, 2, lanes).transpose(0, 2, 1, 3)
    flat = flat.reshape(mode_two * mode_three * 2, lanes)
    flat, a_hbm, c_hbm = (
        pltpu.with_memory_space_constraint(v, pltpu.HBM) for v in (flat, factor_a, factor_c)
    )

    p_other, b_other = contract(jnp.stack([1 - core, x]), flat, a_hbm, c_hbm, half, False)
    p_mine, b_mine = contract(jnp.stack([core, x]), flat, factor_a, factor_c, half, True)
    gram_part = dot(factor_a.T, factor_a)
    gram_part = gram_part + swap(gram_part, "c")
    sent = parcels(b_mine, swap(b_other, "c"))
    got = [sent[0]] + [swap(sent[n], RING, n) for n in (1, 2, 3)]
    column = column_sum(gram_part, swap(gram_part, "xl"), got, depth)
    column = spread(lax.all_to_all(column, "z", 0, 0))
    column, gram_a = flatten(lax.all_to_all(column, "z", 0, 0))
    third, second, first = (swap(column, RING, n) for n in (3, 2, 1))
    columns = [column, first, second, third]
    inverse = inverse_of_product(gram_a, [gram_c])
    f_mine, sums = solve(columns, inverse, p_mine, swap(p_other, "c"))

    sums = sums + swap(sums, "c")
    sums, f_mine = lax.optimization_barrier((sums, f_mine))
    parts = [sums] + [swap(sums, "y", bit) for bit in (1, 2, 3)]
    shape = (4, half // 4, rank)
    f_other = swap(f_mine, "c").reshape(shape)
    factor_b = assemble(jnp.stack([core, x]), f_mine.reshape(shape), f_other)
    parts[0], factor_b = lax.optimization_barrier((parts[0], factor_b))
    plane = ("z", "xl")
    spread_c = collect(parts, lax.axis_size(plane), mode_three)
    shares = lax.all_to_all(spread_c, plane, 0, 0)
    factor_c_new = product(shares, inverse_of_product(gram_a, parts))
    return (factor_b.reshape(mode_two, rank), factor_c_new)


def solution(mesh):
    axes = (mesh.shape["ia"] // 4, 2, 2, mesh.shape["ja"], mesh.shape["ka"])
    fine = Mesh(mesh.devices.reshape(axes), ("z", "xl", "c", "y", "xh"))
    split = ("z", "xl", "c")
    placed = (P("y", "xh", split), P(split, None), P("xh", None), P())
    return jax.shard_map(
        body, mesh=fine, in_specs=placed, out_specs=(P("y", None), P("xh", None)), check_vma=False
    )
```

```python
import functools

import functools

import jax
import jax.numpy as jnp
from jax import lax
from jax.experimental import pallas as pl
from jax.experimental.pallas import tpu as pltpu
from jax.sharding import Mesh, PartitionSpec as P

HIGH = lax.Precision.HIGHEST
F32 = jnp.float32
BF16 = jnp.bfloat16
RING = ("xl", "xh")
VMEM = pl.BlockSpec(memory_space=pltpu.VMEM)
HBM = pl.BlockSpec(memory_space=pltpu.HBM)
SMEM = pl.BlockSpec(memory_space=pltpu.SMEM)


def dot(a, b):
    return jnp.dot(a, b, precision=HIGH, preferred_element_type=F32)


def mxu(a, b):
    return jnp.dot(a, b, preferred_element_type=F32)


def spd_inverse(a, step):
    n = a.shape[0]
    lane = lax.broadcasted_iota(jnp.int32, (step, n), 1)
    row_of = lax.broadcasted_iota(jnp.int32, (step, n), 0)
    lane_all = lax.broadcasted_iota(jnp.int32, (n, n), 1)
    zero = jnp.zeros((step, n), F32)
    for p in range(0, n, step):
        panel = a[p : p + step]
        columns = [jnp.broadcast_to(panel[:, p + c : p + c + 1], (step, n)) for c in range(step)]
        for c in range(step):
            column = columns[c]
            inverse = 1.0 / jnp.broadcast_to(column[c : c + 1], (step, n))
            pivot = row_of == c

            def eliminate(x):
                row = jnp.broadcast_to(x[c : c + 1], (step, n)) * inverse
                return jnp.where(pivot, row, x - column * row)

            panel = eliminate(jnp.where(lane == p + c, jnp.where(pivot, 1.0, 0.0), panel))
            for q in range(c + 1, step):
                columns[q] = eliminate(columns[q])
        spread = [zero] * (p // step) + [panel] + [zero] * ((n - p) // step - 1)
        rest = jnp.where((lane_all >= p) & (lane_all < p + step), 0.0, a)
        rest = rest - dot(a, jnp.concatenate(spread, axis=0))
        pieces = [rest[:p], panel, rest[p + step :]]
        a = jnp.concatenate([x for x in pieces if x.shape[0]], axis=0)
    return a


def total(refs, rows):
    if len(refs) == 1:
        return refs[0][rows]
    first, second, third, fourth = (ref[rows] for ref in refs)
    return (first + second) + (third + fourth)


def collect_kernel(*refs):
    out_ref = refs[-1]
    count, rank = out_ref.shape[1:]
    part = total(refs[:-1], pl.ds(rank, count))
    out_ref[...] = jnp.broadcast_to(part[None], out_ref.shape)


def collect(parts, copies, count):
    rank = parts[0].shape[1]
    return pl.pallas_call(
        collect_kernel,
        out_shape=jax.ShapeDtypeStruct((copies, count, rank), F32),
        in_specs=[VMEM] * 4,
        out_specs=VMEM,
        compiler_params=pltpu.CompilerParams(vmem_limit_bytes=2 << 20),
        name="collect",
    )(*parts)


def inverse_kernel(first_ref, *refs):
    out_ref = refs[-1]
    second = total(refs[:-1], pl.ds(0, first_ref.shape[0]))
    out_ref[...] = spd_inverse(first_ref[...] * second, 16)


def inverse_of_product(first, parts):
    return pl.pallas_call(
        inverse_kernel,
        out_shape=jax.ShapeDtypeStruct(first.shape, F32),
        in_specs=[VMEM] * (1 + len(parts)),
        out_specs=VMEM,
        compiler_params=pltpu.CompilerParams(vmem_limit_bytes=4 << 20),
        cost_estimate=pl.CostEstimate(flops=3 * 10**9, transcendentals=128, bytes_accessed=2**19),
        name="inverse_of_product",
    )(first, *parts)


def gram_kernel(core_ref, a_ref, near_ref, far_ref, g_ref):
    a = a_ref[...]
    rows = near_ref.shape[0]
    g_ref[...] = lax.dot_general(
        a, a, (((0,), (0,)), ((), ())), precision=HIGH, preferred_element_type=F32
    )
    near_ref[...] = g_ref[pl.ds(pl.multiple_of(core_ref[0] * rows, rows), rows)]
    far_ref[...] = g_ref[pl.ds(pl.multiple_of((1 - core_ref[0]) * rows, rows), rows)]


def gram_halves(core, a):
    rank = a.shape[1]
    half = jax.ShapeDtypeStruct((rank // 2, rank), F32)
    return pl.pallas_call(
        gram_kernel,
        out_shape=[half, half],
        in_specs=[SMEM, VMEM],
        out_specs=[VMEM] * 2,
        scratch_shapes=[pltpu.VMEM((rank, rank), F32)],
        compiler_params=pltpu.CompilerParams(vmem_limit_bytes=2 << 20),
        name="gram_halves",
    )(core, a)


def first_inverse_kernel(core_ref, near_ref, far_ref, second_ref, g_ref, out_ref):
    rows = near_ref.shape[0]
    g_ref[pl.ds(pl.multiple_of(core_ref[0] * rows, rows), rows)] = near_ref[...]
    g_ref[pl.ds(pl.multiple_of((1 - core_ref[0]) * rows, rows), rows)] = far_ref[...]
    out_ref[...] = spd_inverse(g_ref[...] * second_ref[...], 16)


def first_inverse(core, near, far, second):
    square = jax.ShapeDtypeStruct(second.shape, F32)
    return pl.pallas_call(
        first_inverse_kernel,
        out_shape=[square, square],
        in_specs=[SMEM] + [VMEM] * 3,
        out_specs=[VMEM] * 2,
        compiler_params=pltpu.CompilerParams(vmem_limit_bytes=4 << 20),
        cost_estimate=pl.CostEstimate(flops=3 * 10**9, transcendentals=128, bytes_accessed=2**19),
        name="first_inverse",
    )(core, near, far, second)


def product_kernel(x_ref, inv_ref, out_ref):
    out_ref[...] = dot(jnp.sum(x_ref[...], axis=0), inv_ref[...])


def product(x, inverse):
    return pl.pallas_call(
        product_kernel,
        out_shape=jax.ShapeDtypeStruct(x.shape[1:], F32),
        in_specs=[VMEM] * 2,
        out_specs=VMEM,
        compiler_params=pltpu.CompilerParams(vmem_limit_bytes=2 << 20),
        name="product",
    )(x, inverse)


def assemble_kernel(at_ref, mine_ref, other_ref, out_ref):
    count = mine_ref.shape[0]
    for n in range(count):
        out_ref[at_ref[0] * count + (at_ref[1] ^ n)] = mine_ref[n]
        out_ref[(1 - at_ref[0]) * count + (at_ref[1] ^ n)] = other_ref[n]


def assemble(at, mine, other):
    return pl.pallas_call(
        assemble_kernel,
        out_shape=jax.ShapeDtypeStruct((2 * mine.shape[0],) + mine.shape[1:], F32),
        in_specs=[SMEM, VMEM, VMEM],
        out_specs=VMEM,
        compiler_params=pltpu.CompilerParams(vmem_limit_bytes=8 << 20),
        name="assemble",
    )(at, mine, other)


def split3(x):
    high = x.astype(BF16)
    rest = x - high.astype(F32)
    middle = rest.astype(BF16)
    return high, middle, (rest - middle.astype(F32)).astype(BF16)


def contract_kernel(chunk, resident, at_ref, x_hbm, a_in, c_in, p_ref, b_ref, *scratch):
    x_ref, w_ref, a_ref, c_ref, sems = scratch
    if resident:
        a_ref, c_ref = a_in, c_in
    count, rows, rank = p_ref.shape
    span = 2 * count
    factors = []
    if not resident:
        for n, (source, target) in enumerate(((a_in, a_ref), (c_in, c_ref))):
            factors.append(pltpu.make_async_copy(source, target, sems.at[rows // chunk + n]))
            factors[n].start()
    part_rows = min(256, chunk)
    copies = []
    for n, at in enumerate(range(0, rows, chunk)):
        size = chunk * span
        block = at_ref[0] * (rows // chunk) + (at_ref[1] ^ n)
        copy = pltpu.make_async_copy(
            x_hbm.at[pl.ds(block * size, size)], x_ref.at[pl.ds(at * span, size)], sems.at[n]
        )
        copy.start()
        copies.append(copy)
    for copy in factors:
        copy.wait()
    for n, part in enumerate(split3(a_ref[...])):
        w_ref[:, n * rank : (n + 1) * rank] = part
    for n, at in enumerate(range(0, rows, chunk)):
        copies[n].wait()
        for row in range(at, at + chunk, part_rows):
            total = None
            for k in range(count):
                x = jnp.concatenate(
                    [
                        x_ref[pl.ds(row * span + k, part_rows, stride=span), :],
                        x_ref[pl.ds(row * span + count + k, part_rows, stride=span), :],
                    ],
                    axis=1,
                )
                high, middle, low = split3(x)
                wide = w_ref[:, : 2 * rank]
                y = mxu(high, wide) + mxu(middle, wide)
                small = mxu(low, w_ref[:, :rank]) + mxu(high, w_ref[:, 2 * rank :])
                value = y[:, :rank] + y[:, rank:] + small
                p_ref[k, row : row + part_rows] = value
                term = value * c_ref[k : k + 1, :]
                total = term if total is None else total + term
            b_ref[row : row + part_rows] = total


def contract(at, x, factor_a, factor_c, rows, resident):
    count, (depth, rank) = factor_c.shape[0], factor_a.shape
    chunk = rows // 4
    return pl.pallas_call(
        functools.partial(contract_kernel, chunk, resident),
        out_shape=[
            jax.ShapeDtypeStruct((count, rows, rank), F32),
            jax.ShapeDtypeStruct((rows, rank), F32),
        ],
        in_specs=[SMEM, HBM] + [VMEM if resident else HBM] * 2,
        out_specs=[VMEM, VMEM],
        scratch_shapes=[
            pltpu.VMEM((rows * 2 * count, depth // 2), F32),
            pltpu.VMEM((depth, 3 * rank), BF16),
            pltpu.VMEM((depth, rank), F32),
            pltpu.VMEM((count, rank), F32),
            pltpu.SemaphoreType.DMA((rows // chunk + 2,)),
        ],
        compiler_params=pltpu.CompilerParams(vmem_limit_bytes=12 << 20),
        cost_estimate=pl.CostEstimate(
            flops=16 * count * rows * depth * rank,
            transcendentals=0,
            bytes_accessed=4 * count * rows * (depth + rank),
        ),
        name="contract",
    )(at, x, factor_a, factor_c)


def parcels_kernel(near_ref, far_ref, *outs):
    block = near_ref.shape[0] // 4
    for n, out in enumerate(outs):
        at = pl.ds(n * block, block)
        out[...] = near_ref[at] + far_ref[at]


def parcels(near, far):
    shape = jax.ShapeDtypeStruct((near.shape[0] // 4, near.shape[1]), F32)
    return pl.pallas_call(
        parcels_kernel,
        out_shape=[shape] * 4,
        in_specs=[VMEM] * 2,
        out_specs=[VMEM] * 4,
        compiler_params=pltpu.CompilerParams(vmem_limit_bytes=6 << 20),
        name="parcels",
    )(near, far)


def column_kernel(g_ref, g_far_ref, *refs):
    out_ref = refs[-1]
    depth = out_ref.shape[0]
    some, few = refs[0].shape[0] // depth, g_ref.shape[0] // depth
    for z in range(depth):
        out_ref[z, :some] = total(refs[:-1], pl.ds(z * some, some))
        at = pl.ds(z * few, few)
        out_ref[z, some:] = g_ref[at] + g_far_ref[at]


def column_sum(gram, gram_far, parts, depth):
    rank = gram.shape[1]
    rows = parts[0].shape[0] + gram.shape[0]
    return pl.pallas_call(
        column_kernel,
        out_shape=jax.ShapeDtypeStruct((depth, rows // depth, rank), F32),
        in_specs=[VMEM] * 6,
        out_specs=VMEM,
        compiler_params=pltpu.CompilerParams(vmem_limit_bytes=2 << 20),
        name="column_sum",
    )(gram, gram_far, *parts)


def spread_kernel(x_ref, out_ref):
    out_ref[...] = jnp.broadcast_to(jnp.sum(x_ref[...], axis=0)[None], out_ref.shape)


def spread(x):
    return pl.pallas_call(
        spread_kernel,
        out_shape=jax.ShapeDtypeStruct(x.shape, F32),
        in_specs=[VMEM],
        out_specs=VMEM,
        compiler_params=pltpu.CompilerParams(vmem_limit_bytes=2 << 20),
        name="spread",
    )(x)


def flatten_kernel(x_ref, m_ref, g_ref):
    depth = x_ref.shape[0]
    some, few = m_ref.shape[0] // depth, g_ref.shape[0] // depth
    for z in range(depth):
        m_ref[z * some : (z + 1) * some] = x_ref[z, :some]
        g_ref[z * few : (z + 1) * few] = x_ref[z, some:]


def flatten(x, count):
    depth, rows, rank = x.shape
    return pl.pallas_call(
        flatten_kernel,
        out_shape=[
            jax.ShapeDtypeStruct((depth * rows - count, rank), F32),
            jax.ShapeDtypeStruct((count, rank), F32),
        ],
        in_specs=[VMEM],
        out_specs=[VMEM] * 2,
        compiler_params=pltpu.CompilerParams(vmem_limit_bytes=2 << 20),
        name="flatten",
    )(x)


def solve_kernel(*refs):
    columns, (inv_ref, p_ref, q_ref, f_ref, out_ref) = refs[:4], refs[4:]
    rank = inv_ref.shape[0]
    block = columns[0].shape[0]
    for n in range(4):
        f = dot(columns[n][...], inv_ref[...])
        f_ref[n * block : (n + 1) * block] = f
    f = f_ref[...]
    out_ref[:rank] = lax.dot_general(
        f, f, (((0,), (0,)), ((), ())), precision=HIGH, preferred_element_type=F32
    )
    out_ref[rank:] = jnp.zeros((out_ref.shape[0] - rank, rank), F32)
    for k in range(p_ref.shape[0]):
        both = (p_ref[k] + q_ref[k]) * f_ref[...]
        out_ref[rank + k : rank + k + 1] = jnp.sum(both, axis=0, keepdims=True)


def solve(columns, inverse, first, second):
    count, rows, rank = first.shape
    return pl.pallas_call(
        solve_kernel,
        out_shape=[
            jax.ShapeDtypeStruct((rows, rank), F32),
            jax.ShapeDtypeStruct((rank + 8 * pl.cdiv(count, 8), rank), F32),
        ],
        in_specs=[VMEM] * 7,
        out_specs=[VMEM] * 2,
        compiler_params=pltpu.CompilerParams(vmem_limit_bytes=12 << 20),
        name="solve",
    )(*columns, inverse, first, second)


def swap(x, axis, bit=1):
    n = lax.axis_size(axis)
    return lax.ppermute(x, axis, [(i, i ^ bit) for i in range(n)])


def body(tensor, factor_a, factor_c, gram_c):
    mode_two, mode_three, mode_one = tensor.shape
    rank = factor_a.shape[1]
    core = lax.axis_index("c").astype(jnp.int32)
    x = lax.axis_index(RING).astype(jnp.int32)
    depth = lax.axis_size("z")
    half = mode_two // 2
    lanes = mode_one // 2
    flat = tensor.reshape(mode_two, mode_three, 2, lanes).transpose(0, 2, 1, 3)
    flat = flat.reshape(mode_two * mode_three * 2, lanes)
    flat, a_hbm, c_hbm = (
        pltpu.with_memory_space_constraint(v, pltpu.HBM) for v in (flat, factor_a, factor_c)
    )

    p_other, b_other = contract(jnp.stack([1 - core, x]), flat, a_hbm, c_hbm, half, False)
    near, far = gram_halves(core.reshape(1), factor_a)
    here, near, far = lax.optimization_barrier((jnp.stack([core, x]), near, far))
    p_mine, b_mine = contract(here, flat, factor_a, factor_c, half, True)
    gram_part = near + swap(far, "c")
    sent = parcels(b_mine, swap(b_other, "c"))
    got = [sent[0]] + [swap(sent[n], RING, n) for n in (1, 2, 3)]
    column = column_sum(gram_part, swap(gram_part, "xl"), got, depth)
    column = spread(lax.all_to_all(column, "z", 0, 0))
    column, near = flatten(lax.all_to_all(column, "z", 0, 0), rank // 2)
    far = swap(near, "c")
    third, second, first = (swap(column, RING, n) for n in (3, 2, 1))
    columns = [column, first, second, third]
    gram_a, inverse = first_inverse(core.reshape(1), near, far, gram_c)
    f_mine, sums = solve(columns, inverse, p_mine, swap(p_other, "c"))

    sums = sums + swap(sums, "c")
    sums, f_mine = lax.optimization_barrier((sums, f_mine))
    parts = [sums] + [swap(sums, "y", bit) for bit in (1, 2, 3)]
    shape = (4, half // 4, rank)
    f_other = swap(f_mine, "c").reshape(shape)
    factor_b = assemble(here, f_mine.reshape(shape), f_other)
    parts[0], factor_b = lax.optimization_barrier((parts[0], factor_b))
    plane = ("z", "xl")
    spread_c = collect(parts, lax.axis_size(plane), mode_three)
    shares = lax.all_to_all(spread_c, plane, 0, 0)
    factor_c_new = product(shares, inverse_of_product(gram_a, parts))
    return (factor_b.reshape(mode_two, rank), factor_c_new)


def solution(mesh):
    axes = (mesh.shape["ia"] // 4, 2, 2, mesh.shape["ja"], mesh.shape["ka"])
    fine = Mesh(mesh.devices.reshape(axes), ("z", "xl", "c", "y", "xh"))
    split = ("z", "xl", "c")
    placed = (P("y", "xh", split), P(split, None), P("xh", None), P())
    return jax.shard_map(
        body, mesh=fine, in_specs=placed, out_specs=(P("y", None), P("xh", None)), check_vma=False
    )
```

```python
import functools

import functools

import jax
import jax.numpy as jnp
from jax import lax
from jax.experimental import pallas as pl
from jax.experimental.pallas import tpu as pltpu
from jax.sharding import Mesh, PartitionSpec as P

HIGH = lax.Precision.HIGHEST
F32 = jnp.float32
BF16 = jnp.bfloat16
RING = ("xl", "xh")
VMEM = pl.BlockSpec(memory_space=pltpu.VMEM)
HBM = pl.BlockSpec(memory_space=pltpu.HBM)
SMEM = pl.BlockSpec(memory_space=pltpu.SMEM)


def dot(a, b):
    return jnp.dot(a, b, precision=HIGH, preferred_element_type=F32)


def mxu(a, b):
    return jnp.dot(a, b, preferred_element_type=F32)


def spd_inverse(a, step):
    n = a.shape[0]
    lane = lax.broadcasted_iota(jnp.int32, (step, n), 1)
    row_of = lax.broadcasted_iota(jnp.int32, (step, n), 0)
    lane_all = lax.broadcasted_iota(jnp.int32, (n, n), 1)
    zero = jnp.zeros((step, n), F32)
    for p in range(0, n, step):
        panel = a[p : p + step]
        columns = [jnp.broadcast_to(panel[:, p + c : p + c + 1], (step, n)) for c in range(step)]
        for c in range(step):
            column = columns[c]
            inverse = 1.0 / jnp.broadcast_to(column[c : c + 1], (step, n))
            pivot = row_of == c

            def eliminate(x):
                row = jnp.broadcast_to(x[c : c + 1], (step, n)) * inverse
                return jnp.where(pivot, row, x - column * row)

            panel = eliminate(jnp.where(lane == p + c, jnp.where(pivot, 1.0, 0.0), panel))
            for q in range(c + 1, step):
                columns[q] = eliminate(columns[q])
        spread = [zero] * (p // step) + [panel] + [zero] * ((n - p) // step - 1)
        rest = jnp.where((lane_all >= p) & (lane_all < p + step), 0.0, a)
        rest = rest - dot(a, jnp.concatenate(spread, axis=0))
        pieces = [rest[:p], panel, rest[p + step :]]
        a = jnp.concatenate([x for x in pieces if x.shape[0]], axis=0)
    return a


def total(refs, rows):
    if len(refs) == 1:
        return refs[0][rows]
    first, second, third, fourth = (ref[rows] for ref in refs)
    return (first + second) + (third + fourth)


def collect_kernel(*refs):
    out_ref = refs[-1]
    count, rank = out_ref.shape[1:]
    part = total(refs[:-1], pl.ds(rank, count))
    out_ref[...] = jnp.broadcast_to(part[None], out_ref.shape)


def collect(parts, copies, count):
    rank = parts[0].shape[1]
    return pl.pallas_call(
        collect_kernel,
        out_shape=jax.ShapeDtypeStruct((copies, count, rank), F32),
        in_specs=[VMEM] * 4,
        out_specs=VMEM,
        compiler_params=pltpu.CompilerParams(vmem_limit_bytes=2 << 20),
        name="collect",
    )(*parts)


def inverse_kernel(first_ref, *refs):
    out_ref = refs[-1]
    second = total(refs[:-1], pl.ds(0, first_ref.shape[0]))
    out_ref[...] = spd_inverse(first_ref[...] * second, 16)


def inverse_of_product(first, parts):
    return pl.pallas_call(
        inverse_kernel,
        out_shape=jax.ShapeDtypeStruct(first.shape, F32),
        in_specs=[VMEM] * (1 + len(parts)),
        out_specs=VMEM,
        compiler_params=pltpu.CompilerParams(vmem_limit_bytes=4 << 20),
        cost_estimate=pl.CostEstimate(flops=3 * 10**9, transcendentals=128, bytes_accessed=2**19),
        name="inverse_of_product",
    )(first, *parts)


def gram_kernel(core_ref, a_ref, near_ref, far_ref, g_ref):
    a = a_ref[...]
    rows = near_ref.shape[0]
    g_ref[...] = lax.dot_general(
        a, a, (((0,), (0,)), ((), ())), precision=HIGH, preferred_element_type=F32
    )
    near_ref[...] = g_ref[pl.ds(pl.multiple_of(core_ref[0] * rows, rows), rows)]
    far_ref[...] = g_ref[pl.ds(pl.multiple_of((1 - core_ref[0]) * rows, rows), rows)]


def gram_halves(core, a):
    rank = a.shape[1]
    half = jax.ShapeDtypeStruct((rank // 2, rank), F32)
    return pl.pallas_call(
        gram_kernel,
        out_shape=[half, half],
        in_specs=[SMEM, VMEM],
        out_specs=[VMEM] * 2,
        scratch_shapes=[pltpu.VMEM((rank, rank), F32)],
        compiler_params=pltpu.CompilerParams(vmem_limit_bytes=2 << 20),
        name="gram_halves",
    )(core, a)


def first_inverse_kernel(core_ref, near_ref, far_ref, second_ref, g_ref, out_ref):
    rows = near_ref.shape[0]
    g_ref[pl.ds(pl.multiple_of(core_ref[0] * rows, rows), rows)] = near_ref[...]
    g_ref[pl.ds(pl.multiple_of((1 - core_ref[0]) * rows, rows), rows)] = far_ref[...]
    out_ref[...] = spd_inverse(g_ref[...] * second_ref[...], 16)


def first_inverse(core, near, far, second):
    square = jax.ShapeDtypeStruct(second.shape, F32)
    return pl.pallas_call(
        first_inverse_kernel,
        out_shape=[square, square],
        in_specs=[SMEM] + [VMEM] * 3,
        out_specs=[VMEM] * 2,
        compiler_params=pltpu.CompilerParams(vmem_limit_bytes=4 << 20),
        cost_estimate=pl.CostEstimate(flops=3 * 10**9, transcendentals=128, bytes_accessed=2**19),
        name="first_inverse",
    )(core, near, far, second)


def product_kernel(x_ref, inv_ref, out_ref):
    out_ref[...] = dot(jnp.sum(x_ref[...], axis=0), inv_ref[...])


def product(x, inverse):
    return pl.pallas_call(
        product_kernel,
        out_shape=jax.ShapeDtypeStruct(x.shape[1:], F32),
        in_specs=[VMEM] * 2,
        out_specs=VMEM,
        compiler_params=pltpu.CompilerParams(vmem_limit_bytes=2 << 20),
        name="product",
    )(x, inverse)


def assemble_kernel(at_ref, mine_ref, other_ref, out_ref):
    count = mine_ref.shape[0]
    for n in range(count):
        out_ref[at_ref[0] * count + (at_ref[1] ^ n)] = mine_ref[n]
        out_ref[(1 - at_ref[0]) * count + (at_ref[1] ^ n)] = other_ref[n]


def assemble(at, mine, other):
    return pl.pallas_call(
        assemble_kernel,
        out_shape=jax.ShapeDtypeStruct((2 * mine.shape[0],) + mine.shape[1:], F32),
        in_specs=[SMEM, VMEM, VMEM],
        out_specs=VMEM,
        compiler_params=pltpu.CompilerParams(vmem_limit_bytes=8 << 20),
        name="assemble",
    )(at, mine, other)


def split3(x):
    high = x.astype(BF16)
    rest = x - high.astype(F32)
    middle = rest.astype(BF16)
    return high, middle, (rest - middle.astype(F32)).astype(BF16)


def contract_kernel(chunk, resident, at_ref, x_hbm, a_in, c_in, p_ref, b_ref, *scratch):
    x_ref, w_ref, a_ref, c_ref, sems = scratch
    if resident:
        a_ref, c_ref = a_in, c_in
    count, rows, rank = p_ref.shape
    span = 2 * count
    factors = []
    if not resident:
        for n, (source, target) in enumerate(((a_in, a_ref), (c_in, c_ref))):
            factors.append(pltpu.make_async_copy(source, target, sems.at[rows // chunk + n]))
            factors[n].start()
    part_rows = min(256, chunk)
    copies = []
    for n, at in enumerate(range(0, rows, chunk)):
        size = chunk * span
        block = at_ref[0] * (rows // chunk) + (at_ref[1] ^ n)
        copy = pltpu.make_async_copy(
            x_hbm.at[pl.ds(block * size, size)], x_ref.at[pl.ds(at * span, size)], sems.at[n]
        )
        copy.start()
        copies.append(copy)
    for copy in factors:
        copy.wait()
    for n, part in enumerate(split3(a_ref[...])):
        w_ref[:, n * rank : (n + 1) * rank] = part
    for n, at in enumerate(range(0, rows, chunk)):
        copies[n].wait()
        for row in range(at, at + chunk, part_rows):
            total = None
            for k in range(count):
                x = jnp.concatenate(
                    [
                        x_ref[pl.ds(row * span + k, part_rows, stride=span), :],
                        x_ref[pl.ds(row * span + count + k, part_rows, stride=span), :],
                    ],
                    axis=1,
                )
                high, middle, low = split3(x)
                wide = w_ref[:, : 2 * rank]
                y = mxu(high, wide) + mxu(middle, wide)
                small = mxu(low, w_ref[:, :rank]) + mxu(high, w_ref[:, 2 * rank :])
                value = y[:, :rank] + y[:, rank:] + small
                p_ref[k, row : row + part_rows] = value
                term = value * c_ref[k : k + 1, :]
                total = term if total is None else total + term
            b_ref[row : row + part_rows] = total


def contract(at, x, factor_a, factor_c, rows, resident):
    count, (depth, rank) = factor_c.shape[0], factor_a.shape
    chunk = rows // 4
    return pl.pallas_call(
        functools.partial(contract_kernel, chunk, resident),
        out_shape=[
            jax.ShapeDtypeStruct((count, rows, rank), F32),
            jax.ShapeDtypeStruct((rows, rank), F32),
        ],
        in_specs=[SMEM, HBM] + [VMEM if resident else HBM] * 2,
        out_specs=[VMEM, VMEM],
        scratch_shapes=[
            pltpu.VMEM((rows * 2 * count, depth // 2), F32),
            pltpu.VMEM((depth, 3 * rank), BF16),
            pltpu.VMEM((depth, rank), F32),
            pltpu.VMEM((count, rank), F32),
            pltpu.SemaphoreType.DMA((rows // chunk + 2,)),
        ],
        compiler_params=pltpu.CompilerParams(vmem_limit_bytes=12 << 20),
        cost_estimate=pl.CostEstimate(
            flops=16 * count * rows * depth * rank,
            transcendentals=0,
            bytes_accessed=4 * count * rows * (depth + rank),
        ),
        name="contract",
    )(at, x, factor_a, factor_c)


def parcels_kernel(near_ref, far_ref, *outs):
    block = near_ref.shape[0] // 4
    for n, out in enumerate(outs):
        at = pl.ds(n * block, block)
        out[...] = near_ref[at] + far_ref[at]


def parcels(near, far):
    shape = jax.ShapeDtypeStruct((near.shape[0] // 4, near.shape[1]), F32)
    return pl.pallas_call(
        parcels_kernel,
        out_shape=[shape] * 4,
        in_specs=[VMEM] * 2,
        out_specs=[VMEM] * 4,
        compiler_params=pltpu.CompilerParams(vmem_limit_bytes=6 << 20),
        name="parcels",
    )(near, far)


def column_kernel(g_ref, g_far_ref, *refs):
    out_ref = refs[-1]
    depth = out_ref.shape[0]
    some, few = refs[0].shape[0] // depth, g_ref.shape[0] // depth
    for z in range(depth):
        out_ref[z, :some] = total(refs[:-1], pl.ds(z * some, some))
        at = pl.ds(z * few, few)
        out_ref[z, some:] = g_ref[at] + g_far_ref[at]


def column_sum(gram, gram_far, parts, depth):
    rank = gram.shape[1]
    rows = parts[0].shape[0] + gram.shape[0]
    return pl.pallas_call(
        column_kernel,
        out_shape=jax.ShapeDtypeStruct((depth, rows // depth, rank), F32),
        in_specs=[VMEM] * 6,
        out_specs=VMEM,
        compiler_params=pltpu.CompilerParams(vmem_limit_bytes=2 << 20),
        name="column_sum",
    )(gram, gram_far, *parts)


def spread_kernel(x_ref, out_ref):
    out_ref[...] = jnp.broadcast_to(jnp.sum(x_ref[...], axis=0)[None], out_ref.shape)


def spread(x):
    return pl.pallas_call(
        spread_kernel,
        out_shape=jax.ShapeDtypeStruct(x.shape, F32),
        in_specs=[VMEM],
        out_specs=VMEM,
        compiler_params=pltpu.CompilerParams(vmem_limit_bytes=2 << 20),
        name="spread",
    )(x)


def flatten_kernel(x_ref, m_ref, g_ref):
    depth = x_ref.shape[0]
    some, few = m_ref.shape[0] // depth, g_ref.shape[0] // depth
    for z in range(depth):
        m_ref[z * some : (z + 1) * some] = x_ref[z, :some]
        g_ref[z * few : (z + 1) * few] = x_ref[z, some:]


def flatten(x, count):
    depth, rows, rank = x.shape
    return pl.pallas_call(
        flatten_kernel,
        out_shape=[
            jax.ShapeDtypeStruct((depth * rows - count, rank), F32),
            jax.ShapeDtypeStruct((count, rank), F32),
        ],
        in_specs=[VMEM],
        out_specs=[VMEM] * 2,
        compiler_params=pltpu.CompilerParams(vmem_limit_bytes=2 << 20),
        name="flatten",
    )(x)


def solve_kernel(*refs):
    own, third, second, first, inv_ref, p_ref, q_ref, f_ref, out_ref = refs
    columns = own, first, second, third
    rank = inv_ref.shape[0]
    block = columns[0].shape[0]
    for n in range(4):
        f = dot(columns[n][...], inv_ref[...])
        f_ref[n * block : (n + 1) * block] = f
    f = f_ref[...]
    out_ref[:rank] = lax.dot_general(
        f, f, (((0,), (0,)), ((), ())), precision=HIGH, preferred_element_type=F32
    )
    out_ref[rank:] = jnp.zeros((out_ref.shape[0] - rank, rank), F32)
    for k in range(p_ref.shape[0]):
        both = (p_ref[k] + q_ref[k]) * f_ref[...]
        out_ref[rank + k : rank + k + 1] = jnp.sum(both, axis=0, keepdims=True)


def solve(columns, inverse, first, second):
    count, rows, rank = first.shape
    return pl.pallas_call(
        solve_kernel,
        out_shape=[
            jax.ShapeDtypeStruct((rows, rank), F32),
            jax.ShapeDtypeStruct((rank + 8 * pl.cdiv(count, 8), rank), F32),
        ],
        in_specs=[VMEM] * 7,
        out_specs=[VMEM] * 2,
        compiler_params=pltpu.CompilerParams(vmem_limit_bytes=12 << 20),
        name="solve",
    )(columns[0], *columns[:0:-1], inverse, first, second)


def swap(x, axis, bit=1):
    n = lax.axis_size(axis)
    return lax.ppermute(x, axis, [(i, i ^ bit) for i in range(n)])


def body(tensor, factor_a, factor_c, gram_c):
    mode_two, mode_three, mode_one = tensor.shape
    rank = factor_a.shape[1]
    core = lax.axis_index("c").astype(jnp.int32)
    x = lax.axis_index(RING).astype(jnp.int32)
    depth = lax.axis_size("z")
    half = mode_two // 2
    lanes = mode_one // 2
    flat = tensor.reshape(mode_two, mode_three, 2, lanes).transpose(0, 2, 1, 3)
    flat = flat.reshape(mode_two * mode_three * 2, lanes)
    flat, a_hbm, c_hbm = (
        pltpu.with_memory_space_constraint(v, pltpu.HBM) for v in (flat, factor_a, factor_c)
    )

    p_other, b_other = contract(jnp.stack([1 - core, x]), flat, a_hbm, c_hbm, half, False)
    near, far = gram_halves(core.reshape(1), factor_a)
    here, near, far = lax.optimization_barrier((jnp.stack([core, x]), near, far))
    p_mine, b_mine = contract(here, flat, factor_a, factor_c, half, True)
    gram_part = near + swap(far, "c")
    sent = parcels(b_mine, swap(b_other, "c"))
    got = [sent[0]] + [swap(sent[n], RING, n) for n in (1, 2, 3)]
    column = column_sum(gram_part, swap(gram_part, "xl"), got, depth)
    column = spread(lax.all_to_all(column, "z", 0, 0))
    column, near = flatten(lax.all_to_all(column, "z", 0, 0), rank // 2)
    far = swap(near, "c")
    third, second, first = (swap(column, RING, n) for n in (3, 2, 1))
    columns = [column, first, second, third]
    gram_a, inverse = first_inverse(core.reshape(1), near, far, gram_c)
    f_mine, sums = solve(columns, inverse, p_mine, swap(p_other, "c"))

    sums = sums + swap(sums, "c")
    sums, f_mine = lax.optimization_barrier((sums, f_mine))
    parts = [sums] + [swap(sums, "y", bit) for bit in (1, 2, 3)]
    shape = (4, half // 4, rank)
    f_other = swap(f_mine, "c").reshape(shape)
    factor_b = assemble(here, f_mine.reshape(shape), f_other)
    parts[0], factor_b = lax.optimization_barrier((parts[0], factor_b))
    plane = ("z", "xl")
    spread_c = collect(parts, lax.axis_size(plane), mode_three)
    shares = lax.all_to_all(spread_c, plane, 0, 0)
    factor_c_new = product(shares, inverse_of_product(gram_a, parts))
    return (factor_b.reshape(mode_two, rank), factor_c_new)


def solution(mesh):
    axes = (mesh.shape["ia"] // 4, 2, 2, mesh.shape["ja"], mesh.shape["ka"])
    fine = Mesh(mesh.devices.reshape(axes), ("z", "xl", "c", "y", "xh"))
    split = ("z", "xl", "c")
    placed = (P("y", "xh", split), P(split, None), P("xh", None), P())
    return jax.shard_map(
        body, mesh=fine, in_specs=placed, out_specs=(P("y", None), P("xh", None)), check_vma=False
    )
```

```python
import functools

import functools

import jax
import jax.numpy as jnp
from jax import lax
from jax.experimental import pallas as pl
from jax.experimental.pallas import tpu as pltpu
from jax.sharding import Mesh, PartitionSpec as P

HIGH = lax.Precision.HIGHEST
F32 = jnp.float32
BF16 = jnp.bfloat16
RING = ("xl", "xh")
VMEM = pl.BlockSpec(memory_space=pltpu.VMEM)
HBM = pl.BlockSpec(memory_space=pltpu.HBM)
SMEM = pl.BlockSpec(memory_space=pltpu.SMEM)


def dot(a, b):
    return jnp.dot(a, b, precision=HIGH, preferred_element_type=F32)


def mxu(a, b):
    return jnp.dot(a, b, preferred_element_type=F32)


def spd_inverse(a, step):
    n = a.shape[0]
    lane = lax.broadcasted_iota(jnp.int32, (step, n), 1)
    row_of = lax.broadcasted_iota(jnp.int32, (step, n), 0)
    lane_all = lax.broadcasted_iota(jnp.int32, (n, n), 1)
    zero = jnp.zeros((step, n), F32)
    for p in range(0, n, step):
        panel = a[p : p + step]
        columns = [jnp.broadcast_to(panel[:, p + c : p + c + 1], (step, n)) for c in range(step)]
        for c in range(step):
            column = columns[c]
            inverse = 1.0 / jnp.broadcast_to(column[c : c + 1], (step, n))
            pivot = row_of == c

            def eliminate(x):
                row = jnp.broadcast_to(x[c : c + 1], (step, n)) * inverse
                return jnp.where(pivot, row, x - column * row)

            panel = eliminate(jnp.where(lane == p + c, jnp.where(pivot, 1.0, 0.0), panel))
            for q in range(c + 1, step):
                columns[q] = eliminate(columns[q])
        spread = [zero] * (p // step) + [panel] + [zero] * ((n - p) // step - 1)
        rest = jnp.where((lane_all >= p) & (lane_all < p + step), 0.0, a)
        rest = rest - dot(a, jnp.concatenate(spread, axis=0))
        pieces = [rest[:p], panel, rest[p + step :]]
        a = jnp.concatenate([x for x in pieces if x.shape[0]], axis=0)
    return a


def total(refs, rows):
    if len(refs) == 1:
        return refs[0][rows]
    first, second, third, fourth = (ref[rows] for ref in refs)
    return (first + second) + (third + fourth)


def collect_kernel(*refs):
    out_ref = refs[-1]
    count, rank = out_ref.shape[1:]
    part = total(refs[:-1], pl.ds(rank, count))
    out_ref[...] = jnp.broadcast_to(part[None], out_ref.shape)


def collect(parts, copies, count):
    rank = parts[0].shape[1]
    return pl.pallas_call(
        collect_kernel,
        out_shape=jax.ShapeDtypeStruct((copies, count, rank), F32),
        in_specs=[VMEM] * 4,
        out_specs=VMEM,
        compiler_params=pltpu.CompilerParams(vmem_limit_bytes=2 << 20),
        name="collect",
    )(*parts)


def inverse_kernel(first_ref, *refs):
    out_ref = refs[-1]
    second = total(refs[:-1], pl.ds(0, first_ref.shape[0]))
    out_ref[...] = spd_inverse(first_ref[...] * second, 16)


def inverse_of_product(first, parts):
    return pl.pallas_call(
        inverse_kernel,
        out_shape=jax.ShapeDtypeStruct(first.shape, F32),
        in_specs=[VMEM] * (1 + len(parts)),
        out_specs=VMEM,
        compiler_params=pltpu.CompilerParams(vmem_limit_bytes=4 << 20),
        cost_estimate=pl.CostEstimate(flops=3 * 10**9, transcendentals=128, bytes_accessed=2**19),
        name="inverse_of_product",
    )(first, *parts)


def gram_kernel(core_ref, a_ref, near_ref, far_ref, g_ref):
    a = a_ref[...]
    rows = near_ref.shape[0]
    g_ref[...] = lax.dot_general(
        a, a, (((0,), (0,)), ((), ())), precision=HIGH, preferred_element_type=F32
    )
    near_ref[...] = g_ref[pl.ds(pl.multiple_of(core_ref[0] * rows, rows), rows)]
    far_ref[...] = g_ref[pl.ds(pl.multiple_of((1 - core_ref[0]) * rows, rows), rows)]


def gram_halves(core, a):
    rank = a.shape[1]
    half = jax.ShapeDtypeStruct((rank // 2, rank), F32)
    return pl.pallas_call(
        gram_kernel,
        out_shape=[half, half],
        in_specs=[SMEM, VMEM],
        out_specs=[VMEM] * 2,
        scratch_shapes=[pltpu.VMEM((rank, rank), F32)],
        compiler_params=pltpu.CompilerParams(vmem_limit_bytes=2 << 20),
        name="gram_halves",
    )(core, a)


def first_inverse_kernel(core_ref, near_ref, far_ref, second_ref, g_ref, out_ref):
    rows = near_ref.shape[0]
    g_ref[pl.ds(pl.multiple_of(core_ref[0] * rows, rows), rows)] = near_ref[...]
    g_ref[pl.ds(pl.multiple_of((1 - core_ref[0]) * rows, rows), rows)] = far_ref[...]
    out_ref[...] = spd_inverse(g_ref[...] * second_ref[...], 16)


def first_inverse(core, near, far, second):
    square = jax.ShapeDtypeStruct(second.shape, F32)
    return pl.pallas_call(
        first_inverse_kernel,
        out_shape=[square, square],
        in_specs=[SMEM] + [VMEM] * 3,
        out_specs=[VMEM] * 2,
        compiler_params=pltpu.CompilerParams(vmem_limit_bytes=4 << 20),
        cost_estimate=pl.CostEstimate(flops=3 * 10**9, transcendentals=128, bytes_accessed=2**19),
        name="first_inverse",
    )(core, near, far, second)


def product_kernel(x_ref, inv_ref, out_ref):
    out_ref[...] = dot(jnp.sum(x_ref[...], axis=0), inv_ref[...])


def product(x, inverse):
    return pl.pallas_call(
        product_kernel,
        out_shape=jax.ShapeDtypeStruct(x.shape[1:], F32),
        in_specs=[VMEM] * 2,
        out_specs=VMEM,
        compiler_params=pltpu.CompilerParams(vmem_limit_bytes=2 << 20),
        name="product",
    )(x, inverse)


def assemble_kernel(at_ref, mine_ref, other_ref, out_ref):
    count = mine_ref.shape[0]
    for n in range(count):
        out_ref[at_ref[0] * count + (at_ref[1] ^ n)] = mine_ref[n]
        out_ref[(1 - at_ref[0]) * count + (at_ref[1] ^ n)] = other_ref[n]


def assemble(at, mine, other):
    return pl.pallas_call(
        assemble_kernel,
        out_shape=jax.ShapeDtypeStruct((2 * mine.shape[0],) + mine.shape[1:], F32),
        in_specs=[SMEM, VMEM, VMEM],
        out_specs=VMEM,
        compiler_params=pltpu.CompilerParams(vmem_limit_bytes=8 << 20),
        name="assemble",
    )(at, mine, other)


def split3(x):
    high = x.astype(BF16)
    rest = x - high.astype(F32)
    middle = rest.astype(BF16)
    return high, middle, (rest - middle.astype(F32)).astype(BF16)


def contract_kernel(chunk, resident, at_ref, x_hbm, a_in, c_in, p_ref, b_ref, *scratch):
    x_ref, w_ref, a_ref, c_ref, sems = scratch
    if resident:
        a_ref, c_ref = a_in, c_in
    count, rows, rank = p_ref.shape
    span = 2 * count
    factors = []
    if not resident:
        for n, (source, target) in enumerate(((a_in, a_ref), (c_in, c_ref))):
            factors.append(pltpu.make_async_copy(source, target, sems.at[rows // chunk + n]))
            factors[n].start()
    part_rows = min(256, chunk)
    copies = []
    for n, at in enumerate(range(0, rows, chunk)):
        size = chunk * span
        block = at_ref[0] * (rows // chunk) + (at_ref[1] ^ n)
        copy = pltpu.make_async_copy(
            x_hbm.at[pl.ds(block * size, size)], x_ref.at[pl.ds(at * span, size)], sems.at[n]
        )
        copy.start()
        copies.append(copy)
    for copy in factors:
        copy.wait()
    for n, part in enumerate(split3(a_ref[...])):
        w_ref[:, n * rank : (n + 1) * rank] = part
    for n, at in enumerate(range(0, rows, chunk)):
        copies[n].wait()
        for row in range(at, at + chunk, part_rows):
            total = None
            for k in range(count):
                x = jnp.concatenate(
                    [
                        x_ref[pl.ds(row * span + k, part_rows, stride=span), :],
                        x_ref[pl.ds(row * span + count + k, part_rows, stride=span), :],
                    ],
                    axis=1,
                )
                high, middle, low = split3(x)
                wide = w_ref[:, : 2 * rank]
                y = mxu(high, wide) + mxu(middle, wide)
                small = mxu(low, w_ref[:, :rank]) + mxu(high, w_ref[:, 2 * rank :])
                value = y[:, :rank] + y[:, rank:] + small
                p_ref[k, row : row + part_rows] = value
                term = value * c_ref[k : k + 1, :]
                total = term if total is None else total + term
            b_ref[row : row + part_rows] = total


def contract(at, x, factor_a, factor_c, rows, resident):
    count, (depth, rank) = factor_c.shape[0], factor_a.shape
    chunk = rows // 4
    return pl.pallas_call(
        functools.partial(contract_kernel, chunk, resident),
        out_shape=[
            jax.ShapeDtypeStruct((count, rows, rank), F32),
            jax.ShapeDtypeStruct((rows, rank), F32),
        ],
        in_specs=[SMEM, HBM] + [VMEM if resident else HBM] * 2,
        out_specs=[VMEM, VMEM],
        scratch_shapes=[
            pltpu.VMEM((rows * 2 * count, depth // 2), F32),
            pltpu.VMEM((depth, 3 * rank), BF16),
            pltpu.VMEM((depth, rank), F32),
            pltpu.VMEM((count, rank), F32),
            pltpu.SemaphoreType.DMA((rows // chunk + 2,)),
        ],
        compiler_params=pltpu.CompilerParams(vmem_limit_bytes=12 << 20),
        cost_estimate=pl.CostEstimate(
            flops=16 * count * rows * depth * rank,
            transcendentals=0,
            bytes_accessed=4 * count * rows * (depth + rank),
        ),
        name="contract",
    )(at, x, factor_a, factor_c)


def parcels_kernel(near_ref, far_ref, *outs):
    block = near_ref.shape[0] // 4
    for n, out in enumerate(outs):
        at = pl.ds(n * block, block)
        out[...] = near_ref[at] + far_ref[at]


def parcels(near, far):
    shape = jax.ShapeDtypeStruct((near.shape[0] // 4, near.shape[1]), F32)
    return pl.pallas_call(
        parcels_kernel,
        out_shape=[shape] * 4,
        in_specs=[VMEM] * 2,
        out_specs=[VMEM] * 4,
        compiler_params=pltpu.CompilerParams(vmem_limit_bytes=6 << 20),
        name="parcels",
    )(near, far)


def column_kernel(g_ref, g_far_ref, *refs):
    out_ref = refs[-1]
    depth = out_ref.shape[0]
    some, few = refs[0].shape[0] // depth, g_ref.shape[0] // depth
    for z in range(depth):
        out_ref[z, :some] = total(refs[:-1], pl.ds(z * some, some))
        at = pl.ds(z * few, few)
        out_ref[z, some:] = g_ref[at] + g_far_ref[at]


def column_sum(gram, gram_far, parts, depth):
    rank = gram.shape[1]
    rows = parts[0].shape[0] + gram.shape[0]
    return pl.pallas_call(
        column_kernel,
        out_shape=jax.ShapeDtypeStruct((depth, rows // depth, rank), F32),
        in_specs=[VMEM] * 6,
        out_specs=VMEM,
        compiler_params=pltpu.CompilerParams(vmem_limit_bytes=2 << 20),
        name="column_sum",
    )(gram, gram_far, *parts)


def spread_kernel(x_ref, out_ref):
    out_ref[...] = jnp.broadcast_to(jnp.sum(x_ref[...], axis=0)[None], out_ref.shape)


def spread(x):
    return pl.pallas_call(
        spread_kernel,
        out_shape=jax.ShapeDtypeStruct(x.shape, F32),
        in_specs=[VMEM],
        out_specs=VMEM,
        compiler_params=pltpu.CompilerParams(vmem_limit_bytes=2 << 20),
        name="spread",
    )(x)


def flatten_kernel(x_ref, m_ref, g_ref):
    depth = x_ref.shape[0]
    some, few = m_ref.shape[0] // depth, g_ref.shape[0] // depth
    for z in range(depth):
        m_ref[z * some : (z + 1) * some] = x_ref[z, :some]
        g_ref[z * few : (z + 1) * few] = x_ref[z, some:]


def flatten(x, count):
    depth, rows, rank = x.shape
    return pl.pallas_call(
        flatten_kernel,
        out_shape=[
            jax.ShapeDtypeStruct((depth * rows - count, rank), F32),
            jax.ShapeDtypeStruct((count, rank), F32),
        ],
        in_specs=[VMEM],
        out_specs=[VMEM] * 2,
        compiler_params=pltpu.CompilerParams(vmem_limit_bytes=2 << 20),
        name="flatten",
    )(x)


def solve_kernel(*refs):
    own, third, second, first, inv_ref, p_ref, q_ref, f_ref, out_ref = refs
    columns = own, first, second, third
    rank = inv_ref.shape[0]
    block = columns[0].shape[0]
    for n in range(4):
        f = dot(columns[n][...], inv_ref[...])
        f_ref[n * block : (n + 1) * block] = f
    f = f_ref[...]
    out_ref[:rank] = lax.dot_general(
        f, f, (((0,), (0,)), ((), ())), precision=HIGH, preferred_element_type=F32
    )
    out_ref[rank:] = jnp.zeros((out_ref.shape[0] - rank, rank), F32)
    for k in range(p_ref.shape[0]):
        both = (p_ref[k] + q_ref[k]) * f_ref[...]
        out_ref[rank + k : rank + k + 1] = jnp.sum(both, axis=0, keepdims=True)


def solve(columns, inverse, first, second):
    count, rows, rank = first.shape
    return pl.pallas_call(
        solve_kernel,
        out_shape=[
            jax.ShapeDtypeStruct((rows, rank), F32),
            jax.ShapeDtypeStruct((rank + 8 * pl.cdiv(count, 8), rank), F32),
        ],
        in_specs=[VMEM] * 7,
        out_specs=[VMEM] * 2,
        compiler_params=pltpu.CompilerParams(vmem_limit_bytes=12 << 20),
        name="solve",
    )(columns[0], *columns[:0:-1], inverse, first, second)


def swap(x, axis, bit=1):
    n = lax.axis_size(axis)
    return lax.ppermute(x, axis, [(i, i ^ bit) for i in range(n)])


def body(tensor, factor_a, factor_c, gram_c):
    mode_two, mode_three, mode_one = tensor.shape
    rank = factor_a.shape[1]
    core = lax.axis_index("c").astype(jnp.int32)
    x = lax.axis_index(RING).astype(jnp.int32)
    depth = lax.axis_size("z")
    half = mode_two // 2
    lanes = mode_one // 2
    flat = tensor.reshape(mode_two, mode_three, 2, lanes).transpose(0, 2, 1, 3)
    flat = flat.reshape(mode_two * mode_three * 2, lanes)
    flat, a_hbm, c_hbm = (
        pltpu.with_memory_space_constraint(v, pltpu.HBM) for v in (flat, factor_a, factor_c)
    )

    p_other, b_other = contract(jnp.stack([1 - core, x]), flat, a_hbm, c_hbm, half, False)
    near, far = gram_halves(core.reshape(1), factor_a)
    here, near, far = lax.optimization_barrier((jnp.stack([core, x]), near, far))
    p_mine, b_mine = contract(here, flat, factor_a, factor_c, half, True)
    gram_part = near + swap(far, "c")
    sent = parcels(b_mine, swap(b_other, "c"))
    got = [sent[0]] + [swap(sent[n], RING, n) for n in (1, 2, 3)]
    column = column_sum(gram_part, swap(gram_part, "xl"), got, depth)
    column = spread(lax.all_to_all(column, "z", 0, 0))
    column, near = flatten(lax.all_to_all(column, "z", 0, 0), rank // 2)
    far = swap(near, "c")
    third, second, first = (swap(column, RING, n) for n in (3, 2, 1))
    columns = [column, first, second, third]
    gram_a, inverse = first_inverse(core.reshape(1), near, far, gram_c)
    f_mine, sums = solve(columns, inverse, p_mine, swap(p_other, "c"))

    sums = sums + swap(sums, "c")
    sums, f_mine = lax.optimization_barrier((sums, f_mine))
    parts = [sums] + [swap(sums, "y", bit) for bit in (1, 3, 2)]
    shape = (4, half // 4, rank)
    f_other = swap(f_mine, "c").reshape(shape)
    factor_b = assemble(here, f_mine.reshape(shape), f_other)
    parts[0], factor_b = lax.optimization_barrier((parts[0], factor_b))
    plane = ("z", "xl")
    spread_c = collect(parts, lax.axis_size(plane), mode_three)
    shares = lax.all_to_all(spread_c, plane, 0, 0)
    factor_c_new = product(shares, inverse_of_product(gram_a, parts))
    return (factor_b.reshape(mode_two, rank), factor_c_new)


def solution(mesh):
    axes = (mesh.shape["ia"] // 4, 2, 2, mesh.shape["ja"], mesh.shape["ka"])
    fine = Mesh(mesh.devices.reshape(axes), ("z", "xl", "c", "y", "xh"))
    split = ("z", "xl", "c")
    placed = (P("y", "xh", split), P(split, None), P("xh", None), P())
    return jax.shard_map(
        body, mesh=fine, in_specs=placed, out_specs=(P("y", None), P("xh", None)), check_vma=False
    )
```
